256 devices in a mesh: lon: 64 (over z_hi, y, x, core), lat: 4 (over z_lo).
Axes of the slice: x: 4, y: 4, z: 8 (z_hi: 2, z_lo: 4; z = z_hi * 4 + z_lo), core: 2. Of those that a mesh axis runs over, the one named last changes fastest.
Arguments:
- fields: float32 [8, 64, 16, 8192], P(None, None, 'lat', 'lon'), may hold values from -6 to 6
- courant: float32 [2, 64, 16, 8192], P(None, None, 'lat', 'lon'), may hold values from -0.5 to 0.5
- cos_zenith: float32 [16, 8192], P('lat', 'lon'), may hold values from 0.2 to 1
- albedo: float32 [16, 8192], P('lat', 'lon'), may hold values from 0.05 to 0.5
- extinction: float32 [14], replicated, may hold values from 0.05 to 4
- single_albedo: float32 [14], replicated, may hold values from 0.2 to 0.95
- band_weight: float32 [14], replicated, may hold values from 0.02 to 0.14
- sun_order: int32 [16, 64, 128], P('lat', 'lon'), may hold values from 0 to 127, each once within a row
- sun_count: int32 [16, 64], P('lat', 'lon'), may hold values from 0 to 128, as said below
Outputs:
- new_fields: float32 [8, 64, 16, 8192], P(None, None, 'lat', 'lon')
- heating: float32 [64, 16, 8192], P(None, 'lat', 'lon')
The draws below stay inside these ranges and needn't reach their ends.
Inputs may be any that keep to these rules, and one draw needn't show every extreme that they name: `sun_count`: for every latitude the counts of tiles t and t + 32 sum to 128.
All inputs are finite; a program needn't handle non-finite values.
Results may differ from the reference program's by a relative error of at most 0.00005.
Values sent between devices are 32-bit elements; how exact they have to be, the bound alone decides.
A program may use at most 128 MiB of HBM per device.

```python
import math
import jax
import jax.numpy as jnp
from jax import lax

FIELDS = 8
BANDS = 14
LEV = 64
LON_DEV = 128
TILES = 64
NLON = 8192
NLAT = 16


def draw_sun_count(key, part):
    tiles = NLON // LON_DEV
    half_tiles = tiles // 2
    key_count = jax.random.fold_in(key, 11)
    key_side = jax.random.fold_in(key, 23)
    counts = jax.random.randint(key_count, (NLAT, half_tiles), LON_DEV // 2, LON_DEV + 1)
    counts = counts.at[0, 0].set(LON_DEV)
    side = jax.random.randint(key_side, (NLAT, half_tiles), 0, 2)
    first = jnp.where(side == 1, counts, LON_DEV - counts)
    second = LON_DEV - first
    return jnp.concatenate([first, second], axis=1).astype(jnp.int32)


def level_of(stream_key, dims, split, least, high):
    gain = 1.0
    for position, shards_of in split:
        draws = jax.random.uniform(jax.random.fold_in(jax.random.fold_in(stream_key, 6), position), (shards_of,), jnp.float32, least / len(split), high / len(split))
        gain = gain * jnp.repeat(jnp.exp(draws), dims[position] // shards_of).reshape((-1,) + (1,) * (len(dims) - 1 - position))
    return gain


def scatter_about(key, extent, spread, reach, cuts=(), held_as=jnp.bfloat16):
    entries = jax.random.normal(key, extent, jnp.float32) * spread
    if len(cuts) > 0:
        entries = level_of(key, extent, cuts, -0.22, 0.18) * entries
    return jnp.clip(entries, min=-reach, max=reach).astype(held_as)


def setup_inputs(seed: int = 0) -> dict:
    key_of = jax.random.split(jax.random.key(seed), 10)
    return {
        "fields": scatter_about(key_of[0], (FIELDS, LEV, NLAT, NLON), 1.0, 6.0, ((2, 4), (3, 64)), jnp.float32),
        "courant": jnp.clip(jax.random.uniform(key_of[1], (2, LEV, NLAT, NLON), jnp.float32, -0.5, 0.5) * level_of(key_of[1], (2, LEV, NLAT, NLON), ((2, 4), (3, 64)), -0.4, 0.0), -0.5, 0.5),
        "cos_zenith": jnp.clip(0.2 + 0.8 * jax.random.uniform(key_of[2], (NLAT, NLON), jnp.float32) ** level_of(key_of[2], (NLAT, NLON), ((0, 4), (1, 64)), -0.2, 0.2), 0.2, 1.0),
        "albedo": jnp.clip(0.05 + 0.45 * jax.random.uniform(key_of[3], (NLAT, NLON), jnp.float32) ** level_of(key_of[3], (NLAT, NLON), ((0, 4), (1, 64)), -0.2, 0.2), 0.05, 0.5),
        "extinction": jnp.clip(jnp.exp(jax.random.uniform(key_of[4], (BANDS,), jnp.float32, math.log(0.05), math.log(4.0))), 0.05, 4.0),
        "single_albedo": jnp.clip(jax.random.uniform(key_of[5], (BANDS,), jnp.float32, 0.2, 0.95), 0.2, 0.95),
        "band_weight": jnp.clip(jax.random.uniform(key_of[6], (BANDS,), jnp.float32, 0.02, 0.14), 0.02, 0.14),
        "sun_order": jax.vmap(lambda own: jax.random.permutation(own, LON_DEV))(jax.random.split(key_of[7], NLAT * TILES)).reshape((NLAT, TILES, LON_DEV)).astype(jnp.int32),
        "sun_count": draw_sun_count(jax.random.fold_in(key_of[9], 71), 0),
    }


def tendency(field, east_num, north_num):
    right = jnp.roll(field, -1, axis=2)
    left = jnp.roll(field, 1, axis=2)
    right_two = jnp.roll(field, -2, axis=2)
    east = east_num * (7.0 * (field + right) - (left + right_two)) / 12.0
    div_east = east - jnp.roll(east, 1, axis=2)
    padded = jnp.pad(field, ((0, 0), (2, 2), (0, 0)))
    north = north_num * (7.0 * (padded[:, 2:-2] + padded[:, 3:-1]) - (padded[:, 1:-3] + padded[:, 4:])) / 12.0
    shifted = jnp.concatenate([jnp.zeros_like(north[:, :1]), north[:, :-1]], axis=1)
    div_north = north - shifted
    return -(div_east + div_north)


def optics(water, cosz, extinction, single_albedo):
    levels = water.shape[0]
    tau = (extinction * (4.0 / levels))[None, :, None] * water[:, None, :]
    depth = jnp.cumsum(tau, axis=0)
    mu = cosz[None, None, :]
    s_top = jnp.exp(-(depth - tau) / mu)
    s_bot = jnp.exp(-depth / mu)
    direct = jnp.exp(-tau / mu)
    decay = jnp.exp(-1.66 * tau)
    scat = 0.5 * single_albedo[None, :, None] * (1.0 - decay)
    transmit = decay + scat
    source = 0.5 * single_albedo[None, :, None] * mu * s_top * (1.0 - direct)
    return scat, transmit, source, s_top, s_bot


def up_step(carry, layer):
    a_below, b_below = carry
    reflect, transmit, source = layer
    den = 1.0 - reflect * a_below
    a_here = reflect + transmit * transmit * a_below / den
    b_here = transmit * (a_below * source + b_below) / den + source
    return (a_here, b_here), (a_here, b_here, den, b_below)


def down_step(d_top, layer):
    transmit, reflect, source, den, b_below = layer
    d_bot = (transmit * d_top + reflect * b_below + source) / den
    return d_bot, d_top


def radiate(water, cosz, surface, extinction, single_albedo, band_weight):
    reflect, transmit, source, s_top, s_bot = optics(water, cosz, extinction, single_albedo)
    mu = cosz[None, :]
    a_floor = jnp.broadcast_to(surface[None, :], reflect.shape[1:])
    b_floor = a_floor * mu * s_bot[-1]
    _, (a_all, b_all, den_all, b_next) = lax.scan(up_step, (a_floor, b_floor), (reflect, transmit, source), reverse=True)
    d_floor, d_all = lax.scan(down_step, jnp.zeros_like(a_floor), (transmit, reflect, source, den_all, b_next))
    net_top = mu[None] * s_top + d_all - (a_all * d_all + b_all)
    net_floor = mu * s_bot[-1] + d_floor - (a_floor * d_floor + b_floor)
    net_bot = jnp.concatenate([net_top[1:], net_floor[None]], axis=0)
    absorbed = net_top - net_bot
    return water.shape[0] * jnp.sum(absorbed * band_weight[None, :, None], axis=1)


def reference(fields, courant, cos_zenith, albedo, extinction, single_albedo, band_weight, sun_order, sun_count):
    east_num = courant[0]
    north_num = courant[1]

    def advance(field):
        section = field + tendency(field, east_num, north_num)
        return 0.5 * ((field + section) + tendency(section, east_num, north_num))

    advanced = lax.map(advance, fields)
    inverse = jnp.argsort(sun_order, axis=-1).astype(jnp.int32)
    sunlit = (inverse < sun_count[:, :, None]).astype(jnp.float32).reshape(NLAT, NLON)
    water = jax.nn.softplus(fields[1])
    tiles = NLON // LON_DEV

    def by_tile(array):
        lead = array.shape[0]
        return array.reshape(lead, NLAT, tiles, LON_DEV).transpose(2, 0, 1, 3).reshape(tiles, lead, NLAT * LON_DEV)

    packed = by_tile(jnp.concatenate([water, cos_zenith[None], albedo[None]], axis=0))

    def one_tile(block):
        return radiate(block[:LEV], block[LEV], block[LEV + 1], extinction, single_albedo, band_weight)

    heat_tiles = lax.map(one_tile, packed)
    heat_all = heat_tiles.reshape(tiles, LEV, NLAT, LON_DEV).transpose(1, 2, 0, 3).reshape(LEV, NLAT, NLON)
    heating = heat_all * sunlit[None]
    new_fields = jnp.concatenate([advanced[:1] + 0.5 * heating[None], advanced[1:]], axis=0)
    return new_fields, heating
```

```python
import functools

import jax
import jax.numpy as jnp
from jax import lax
from jax.experimental import pallas as pl
from jax.experimental.pallas import tpu as pltpu
from jax.sharding import PartitionSpec as P

MESH = pl.DeviceIdType.MESH
HALO = 2


def step_kernel(
    dims,
    fields_hbm,
    flat_hbm,
    courant_hbm,
    cosz_ref,
    albedo_ref,
    ext_ref,
    ssa_ref,
    weight_ref,
    order_ref,
    count_ref,
    out_hbm,
    heat_hbm,
    q_buf,
    s_buf,
    o_buf,
    c_east,
    c_west,
    c_north,
    water_buf,
    heat_buf,
    rad_a,
    rad_b,
    rad_c,
    rad_g,
    pack_own,
    pack_send,
    pack_recv,
    own_sem,
    out_sem,
    z1_send,
    z1_recv,
    z2_send,
    z2_recv,
    cn_send,
    cn_recv,
    x_send,
    x_recv,
):
    nf, lev, rows, lanes, bands, n_lat, n_lon = dims
    groups = lev // 8
    pairs = bands // 2
    lat = lax.axis_index("lat")
    lon = lax.axis_index("lon")
    has_up = lat < n_lat - 1
    has_dn = lat > 0
    right = lax.rem(lon + 1, n_lon)
    left = lax.rem(lon + n_lon - 1, n_lon)
    up_id = {"lon": lon, "lat": lat + 1}
    dn_id = {"lon": lon, "lat": lat - 1}
    right_id = {"lon": right, "lat": lat}
    left_id = {"lon": left, "lat": lat}

    water_copy = pltpu.make_async_copy(flat_hbm.at[1], water_buf, own_sem.at[0])
    water_copy.start()
    courant_copies = []
    for r in range(rows):
        courant_copies.append(
            pltpu.make_async_copy(courant_hbm.at[0, :, r, 0], c_east.at[r], own_sem.at[1 + r])
        )
        courant_copies.append(
            pltpu.make_async_copy(
                courant_hbm.at[1, :, r, 0], c_north.at[r + 1], own_sem.at[1 + rows + r]
            )
        )
    for copy in courant_copies:
        copy.start()
    base = 1 + 2 * rows

    def own_copy(f, r):
        return pltpu.make_async_copy(
            fields_hbm.at[f, :, r, 0], q_buf.at[f, HALO + r], own_sem.at[base + f * rows + r]
        )

    for f in range(nf):
        for r in range(rows):
            own_copy(f, r).start()

    barrier = pltpu.get_barrier_semaphore()
    pl.semaphore_signal(barrier, inc=1, device_id=right_id, device_id_type=MESH)
    pl.semaphore_signal(barrier, inc=1, device_id=left_id, device_id_type=MESH)

    @pl.when(has_up)
    def _():
        pl.semaphore_signal(barrier, inc=1, device_id=up_id, device_id_type=MESH)

    @pl.when(has_dn)
    def _():
        pl.semaphore_signal(barrier, inc=1, device_id=dn_id, device_id_type=MESH)

    pl.semaphore_wait(barrier, 2 + has_up.astype(jnp.int32) + has_dn.astype(jnp.int32))

    def z1_copy(f, side, r):
        if side == 0:
            source, target, device = rows - HALO + r, r, up_id
        else:
            source, target, device = r, HALO + rows + r, dn_id
        return pltpu.make_async_remote_copy(
            src_ref=fields_hbm.at[f, :, source, 0],
            dst_ref=q_buf.at[f, target],
            send_sem=z1_send.at[side, f, r],
            recv_sem=z1_recv.at[side, f, r],
            device_id=device,
            device_id_type=MESH,
        )

    def z2_copy(f, side):
        if side == 0:
            source, target, device = rows, 0, up_id
        else:
            source, target, device = HALO, HALO + rows, dn_id
        return pltpu.make_async_remote_copy(
            src_ref=s_buf.at[f, pl.ds(source, HALO)],
            dst_ref=s_buf.at[f, pl.ds(target, HALO)],
            send_sem=z2_send.at[side, f],
            recv_sem=z2_recv.at[side, f],
            device_id=device,
            device_id_type=MESH,
        )

    cn_copy = pltpu.make_async_remote_copy(
        src_ref=courant_hbm.at[1, :, rows - 1, 0],
        dst_ref=c_north.at[0],
        send_sem=cn_send,
        recv_sem=cn_recv,
        device_id=up_id,
        device_id_type=MESH,
    )

    def x_copy(n, side):
        return pltpu.make_async_remote_copy(
            src_ref=pack_send.at[side, n],
            dst_ref=pack_recv.at[side, n],
            send_sem=x_send.at[side, n],
            recv_sem=x_recv.at[side, n],
            device_id=right_id if side == 0 else left_id,
            device_id_type=MESH,
        )

    @pl.when(has_up)
    def _():
        cn_copy.start()

    @pl.loop(0, nf)
    def _(f):
        @pl.when(has_up)
        def _():
            for r in range(HALO):
                z1_copy(f, 0, r).start()

        @pl.when(has_dn)
        def _():
            for r in range(HALO):
                z1_copy(f, 1, r).start()

    zero = jnp.zeros((8, lanes), jnp.float32)

    def fill_zero(ref):
        for g in range(groups):
            ref[pl.ds(8 * g, 8), :] = zero

    @pl.when(jnp.logical_not(has_dn))
    def _():
        fill_zero(c_north.at[0])

        @pl.loop(0, nf)
        def _(f):
            for r in range(HALO):
                fill_zero(q_buf.at[f, r])
                fill_zero(s_buf.at[f, r])

    @pl.when(jnp.logical_not(has_up))
    def _():
        @pl.loop(0, nf)
        def _(f):
            for r in range(HALO):
                fill_zero(q_buf.at[f, HALO + rows + r])
                fill_zero(s_buf.at[f, HALO + rows + r])

    lane = lax.broadcasted_iota(jnp.int32, (8, lanes), 1)
    sub = lax.broadcasted_iota(jnp.int32, (8, lanes), 0)
    slot = lane >> 2
    own_half = (lane & 3) < 2
    low = sub < 4

    def pack(load):
        packed = zero
        for r in range(rows):
            for g in range(groups):
                k = r * groups + g
                packed = jnp.where(
                    slot == k, pltpu.roll(load(r, g), (4 * k + 2) % lanes, 1), packed
                )
        return packed

    def send_pair(n, even, odd):
        pack_send[0, n] = jnp.where(own_half, even, pltpu.roll(odd, 2, 1))
        pack_send[1, n] = jnp.where(own_half, pltpu.roll(even, lanes - 2, 1), odd)

    def recv_pair(n, odd):
        from_left = pack_recv[0, n]
        from_right = pack_recv[1, n]
        first = jnp.where(own_half, from_left, pltpu.roll(from_right, 2, 1))
        second = jnp.where(own_half, pltpu.roll(from_left, lanes - 2, 1), from_right)
        return jnp.where(odd, second, first)

    for copy in courant_copies:
        copy.wait()

    @pl.loop(0, nf)
    def _(f):
        for r in range(rows):
            own_copy(f, r).wait()
        pack_own[f] = pack(lambda r, g: q_buf[f, HALO + r, pl.ds(8 * g, 8), :])

    pairs_f = nf // 2
    c_slot = 2 * pairs_f
    c_pack = pack(lambda r, g: c_east[r, pl.ds(8 * g, 8), :])
    for n in range(pairs_f):
        send_pair(n, pack_own[2 * n], pack_own[2 * n + 1])
    send_pair(c_slot, c_pack, c_pack)
    for n in list(range(pairs_f)) + [c_slot]:
        x_copy(n, 0).start()
        x_copy(n, 1).start()

    cosz = jnp.concatenate([cosz_ref[...], cosz_ref[...]], axis=0)
    albedo = jnp.concatenate([albedo_ref[...], albedo_ref[...]], axis=0)
    neg_inv_mu = -1.0 / cosz
    ext = [
        jnp.where(low, ext_ref[2 * p], ext_ref[2 * p + 1]) * (4.0 / lev) for p in range(pairs)
    ]
    half_ssa = [jnp.where(low, ssa_ref[2 * p], ssa_ref[2 * p + 1]) * 0.5 for p in range(pairs)]
    weight = [jnp.where(low, weight_ref[2 * p], weight_ref[2 * p + 1]) for p in range(pairs)]

    ranks = lax.broadcasted_iota(jnp.int32, (lanes, lanes), 1)
    columns = lax.broadcasted_iota(jnp.int32, (lanes, lanes), 0)
    ones = jnp.ones((8, lanes), jnp.float32)
    sunlit = zero
    for r in range(rows):
        hit = (order_ref[r] == columns) & (ranks < count_ref[r, 0])
        row = lax.dot_general(
            ones,
            hit.astype(jnp.float32),
            (((1,), (1,)), ((), ())),
            preferred_element_type=jnp.float32,
        )
        sunlit = jnp.where((sub & 3) == r, row, sunlit)
    sunlit = sunlit * float(lev)

    water_copy.wait()

    def optics(k, beam):
        raw = water_buf[pl.ds(pl.multiple_of(8 * k, 8), 8), :]
        water = jnp.maximum(raw, 0.0) + jnp.log1p(jnp.exp(-jnp.abs(raw)))
        turned = pltpu.roll(water, 4, 0)
        for half in range(2):
            level = 2 * k + half
            here = jnp.where(low, water, turned) if half == 0 else jnp.where(low, turned, water)
            after = []
            for p in range(pairs):
                tau = ext[p] * here
                direct = jnp.exp(tau * neg_inv_mu)
                decay = jnp.exp(tau * -1.66)
                rad_a[level, p] = decay
                rad_b[level, p] = half_ssa[p] * (beam[p] * (1.0 - direct))
                rad_g[level, p] = beam[p]
                after.append(beam[p] * direct)
            beam = tuple(after)
        return beam

    beam = lax.fori_loop(0, lev // 2, optics, tuple(cosz for _ in range(pairs)))

    def up_level(i, carry):
        level = lev - 1 - i
        a_below, b_below = carry
        a_out, b_out = [], []
        for p in range(pairs):
            decay = rad_a[level, p]
            source = rad_b[level, p]
            reflect = half_ssa[p] * (1.0 - decay)
            transmit = decay + reflect
            inv = 1.0 / (1.0 - reflect * a_below[p])
            through = transmit * inv
            a_here = reflect + transmit * through * a_below[p]
            b_here = through * (a_below[p] * source + b_below[p]) + source
            rad_a[level, p] = through
            rad_b[level, p] = (reflect * b_below[p] + source) * inv
            rad_c[level, p] = weight[p] * (1.0 - a_here)
            rad_g[level, p] = weight[p] * (rad_g[level, p] - b_here)
            a_out.append(a_here)
            b_out.append(b_here)
        return tuple(a_out), tuple(b_out)

    floor_b = tuple(albedo * beam[p] for p in range(pairs))
    for p in range(pairs):
        rad_c[lev, p] = weight[p] * (1.0 - albedo)
        rad_g[lev, p] = weight[p] * (beam[p] - floor_b[p])
    lax.fori_loop(0, lev, up_level, (tuple(albedo for _ in range(pairs)), floor_b))

    def net_flux(level, down):
        total = rad_c[level, 0] * down[0] + rad_g[level, 0]
        for p in range(1, pairs):
            total = total + (rad_c[level, p] * down[p] + rad_g[level, p])
        return total + pltpu.roll(total, 4, 0)

    def down_pair(k, carry):
        down, net = carry
        heats = []
        for half in range(2):
            level = 2 * k + half
            down = tuple(rad_a[level, p] * down[p] + rad_b[level, p] for p in range(pairs))
            below = net_flux(level + 1, down)
            heats.append((net - below) * sunlit)
            net = below
        heat_buf[pl.ds(pl.multiple_of(8 * k, 8), 8), :] = jnp.where(low, heats[0], heats[1])
        return down, net

    start = tuple(zero for _ in range(pairs))
    lax.fori_loop(0, lev // 2, down_pair, (start, net_flux(0, start)))
    heat_copy = pltpu.make_async_copy(heat_buf, heat_hbm, out_sem.at[nf * rows])
    heat_copy.start()

    def x_wait(n):
        x_copy(n, 0).wait_recv()
        x_copy(n, 1).wait_recv()

    x_wait(c_slot)

    @pl.when(has_dn)
    def _():
        cn_copy.wait_recv()

    c_halo = recv_pair(c_slot, False)
    for r in range(rows):
        for g in range(groups):
            k = r * groups + g
            here = c_east[r, pl.ds(8 * g, 8), :]
            edge = pltpu.roll(c_halo, (lanes - 2 - 4 * k) % lanes, 1)
            west = pltpu.roll(jnp.where(lane == lanes - 1, edge, here), 1, 1)
            c_west[r, pl.ds(8 * g, 8), :] = west * (1.0 / 12.0)
            c_east[r, pl.ds(8 * g, 8), :] = here * (1.0 / 12.0)
    for r in range(rows + 1):
        for g in range(groups):
            c_north[r, pl.ds(8 * g, 8), :] = c_north[r, pl.ds(8 * g, 8), :] * (1.0 / 12.0)

    first_lane = lane == 0
    first_two = lane < 2
    last_lane = lane == lanes - 1
    last_two = lane >= lanes - 2

    def tendency(buf, f, halo, emit):
        for g in range(groups):
            at = pl.ds(8 * g, 8)
            q = [buf[f, j, at, :] for j in range(rows + 2 * HALO)]
            north = [
                c_north[j, at, :] * (7.0 * (q[j + 1] + q[j + 2]) - (q[j] + q[j + 3]))
                for j in range(rows + 1)
            ]
            for r in range(rows):
                k = r * groups + g
                here = q[r + HALO]
                edge = pltpu.roll(halo, (lanes - 2 - 4 * k) % lanes, 1)
                r1 = pltpu.roll(jnp.where(first_lane, edge, here), lanes - 1, 1)
                r2 = pltpu.roll(jnp.where(first_two, edge, here), lanes - 2, 1)
                l1 = pltpu.roll(jnp.where(last_lane, edge, here), 1, 1)
                l2 = pltpu.roll(jnp.where(last_two, edge, here), 2, 1)
                east = c_east[r, at, :] * (7.0 * (here + r1) - (l1 + r2))
                west = c_west[r, at, :] * (7.0 * (l1 + here) - (l2 + r1))
                emit(r, g, here, -((east - west) + (north[r + 1] - north[r])))

    def z1_wait(f):
        @pl.when(has_dn)
        def _():
            for r in range(HALO):
                z1_copy(f, 0, r).wait_recv()

        @pl.when(has_up)
        def _():
            for r in range(HALO):
                z1_copy(f, 1, r).wait_recv()

    for n in range(pairs_f):
        x_wait(n)

    @pl.loop(0, pairs_f)
    def _(n):
        packed = []
        for odd in range(2):
            f = 2 * n + odd
            z1_wait(f)

            def emit(r, g, here, change):
                s_buf[f, HALO + r, pl.ds(8 * g, 8), :] = here + change

            tendency(q_buf, f, recv_pair(n, odd == 1), emit)
            packed.append(pack(lambda r, g: s_buf[f, HALO + r, pl.ds(8 * g, 8), :]))

            @pl.when(has_up)
            def _():
                z2_copy(f, 0).start()

            @pl.when(has_dn)
            def _():
                z2_copy(f, 1).start()

        m = pairs_f + n
        send_pair(m, packed[0], packed[1])
        x_copy(m, 0).start()
        x_copy(m, 1).start()

    def out_copy(f, r):
        return pltpu.make_async_copy(
            o_buf.at[f, r], out_hbm.at[f, :, r, 0], out_sem.at[f * rows + r]
        )

    def final(f, halo, extra):
        def emit(r, g, here, change):
            value = 0.5 * ((q_buf[f, HALO + r, pl.ds(8 * g, 8), :] + here) + change)
            if extra:
                value = value + 0.5 * heat_buf[pl.ds(8 * rows * g + r, 8, stride=rows), :]
            o_buf[f, r, pl.ds(8 * g, 8), :] = value

        @pl.when(has_dn)
        def _():
            z2_copy(f, 0).wait_recv()

        @pl.when(has_up)
        def _():
            z2_copy(f, 1).wait_recv()

        tendency(s_buf, f, halo, emit)
        for r in range(rows):
            out_copy(f, r).start()

    x_wait(pairs_f)
    final(0, recv_pair(pairs_f, False), True)

    @pl.loop(1, nf)
    def _(f):
        n = pairs_f + f // 2

        @pl.when(f % 2 == 0)
        def _():
            x_wait(n)

        final(f, recv_pair(n, f % 2 == 1), False)

    heat_copy.wait()

    @pl.loop(0, nf)
    def _(f):
        for r in range(rows):
            out_copy(f, r).wait()

        @pl.when(has_up)
        def _():
            for r in range(HALO):
                z1_copy(f, 0, r).wait_send()
            z2_copy(f, 0).wait_send()

        @pl.when(has_dn)
        def _():
            for r in range(HALO):
                z1_copy(f, 1, r).wait_send()
            z2_copy(f, 1).wait_send()

    @pl.when(has_up)
    def _():
        cn_copy.wait_send()

    for n in range(2 * pairs_f + 1):
        x_copy(n, 0).wait_send()
        x_copy(n, 1).wait_send()


def per_device(n_lat, n_lon, fields, courant, cosz, albedo, ext, ssa, weight, order, count):
    nf, lev, rows, lanes = fields.shape
    bands = ext.shape[0]
    dims = (nf, lev, rows, lanes, bands, n_lat, n_lon)
    tall = rows + 2 * HALO
    f32 = jnp.float32
    any_spec = pl.BlockSpec(memory_space=pl.ANY)
    vmem_spec = pl.BlockSpec(memory_space=pltpu.VMEM)
    smem_spec = pl.BlockSpec(memory_space=pltpu.SMEM)
    rad = pltpu.VMEM((lev + 1, bands // 2, 8, lanes), f32)
    packs = nf + 1
    out, heat = pl.pallas_call(
        functools.partial(step_kernel, dims),
        out_shape=(
            jax.ShapeDtypeStruct((nf, lev, rows, 1, lanes), f32),
            jax.ShapeDtypeStruct((lev * rows, lanes), f32),
        ),
        in_specs=[any_spec] * 3
        + [vmem_spec] * 2
        + [smem_spec] * 3
        + [vmem_spec, smem_spec],
        out_specs=(any_spec, any_spec),
        scratch_shapes=[
            pltpu.VMEM((nf, tall, lev, lanes), f32),
            pltpu.VMEM((nf, tall, lev, lanes), f32),
            pltpu.VMEM((nf, rows, lev, lanes), f32),
            pltpu.VMEM((rows, lev, lanes), f32),
            pltpu.VMEM((rows, lev, lanes), f32),
            pltpu.VMEM((rows + 1, lev, lanes), f32),
            pltpu.VMEM((lev * rows, lanes), f32),
            pltpu.VMEM((lev * rows, lanes), f32),
            rad,
            rad,
            rad,
            rad,
            pltpu.VMEM((nf, 8, lanes), f32),
            pltpu.VMEM((2, packs, 8, lanes), f32),
            pltpu.VMEM((2, packs, 8, lanes), f32),
            pltpu.SemaphoreType.DMA((1 + 2 * rows + nf * rows,)),
            pltpu.SemaphoreType.DMA((nf * rows + 1,)),
            pltpu.SemaphoreType.DMA((2, nf, HALO)),
            pltpu.SemaphoreType.DMA((2, nf, HALO)),
            pltpu.SemaphoreType.DMA((2, nf)),
            pltpu.SemaphoreType.DMA((2, nf)),
            pltpu.SemaphoreType.DMA,
            pltpu.SemaphoreType.DMA,
            pltpu.SemaphoreType.DMA((2, packs)),
            pltpu.SemaphoreType.DMA((2, packs)),
        ],
        compiler_params=pltpu.CompilerParams(
            collective_id=0, has_side_effects=True, vmem_limit_bytes=48 * 1024 * 1024
        ),
        name="advect_radiate",
    )(
        fields.reshape(nf, lev, rows, 1, lanes),
        fields.reshape(nf, lev * rows, lanes),
        courant.reshape(2, lev, rows, 1, lanes),
        cosz,
        albedo,
        ext,
        ssa,
        weight,
        order,
        count,
    )
    return out.reshape(nf, lev, rows, lanes), heat.reshape(lev, rows, lanes)


def solution(mesh):
    n_lat, n_lon = mesh.shape["lat"], mesh.shape["lon"]
    in_specs = (
        P(None, None, "lat", "lon"),
        P(None, None, "lat", "lon"),
        P("lat", "lon"),
        P("lat", "lon"),
        P(),
        P(),
        P(),
        P("lat", "lon", None),
        P("lat", "lon"),
    )
    out_specs = (P(None, None, "lat", "lon"), P(None, "lat", "lon"))
    return jax.shard_map(
        functools.partial(per_device, n_lat, n_lon),
        mesh=mesh,
        in_specs=in_specs,
        out_specs=out_specs,
        check_vma=False,
    )
```

```python
import functools

import jax
import jax.numpy as jnp
from jax import lax
from jax.experimental import pallas as pl
from jax.experimental.pallas import tpu as pltpu
from jax.sharding import PartitionSpec as P

MESH = pl.DeviceIdType.MESH
HALO = 2


def step_kernel(
    dims,
    fields_hbm,
    flat_hbm,
    courant_hbm,
    c_flat_hbm,
    cosz_hbm,
    albedo_hbm,
    ext_hbm,
    ssa_hbm,
    weight_hbm,
    order_hbm,
    count_hbm,
    out_ref,
    heat_ref,
    q_buf,
    q_halo,
    s_buf,
    c_buf,
    c_east,
    c_west,
    c_north,
    cosz_ref,
    albedo_ref,
    ext_ref,
    ssa_ref,
    weight_ref,
    order_ref,
    count_ref,
    rad_a,
    rad_b,
    rad_c,
    rad_g,
    pack_own,
    pack_send,
    pack_recv,
    own_sem,
    small_sem,
    go_sem,
    z1_send,
    z1_recv,
    z2_send,
    z2_recv,
    cn_send,
    cn_recv,
    x_send,
    x_recv,
):
    nf, lev, rows, lanes, bands, n_lat, n_lon = dims
    groups = lev // 8
    pairs = bands // 2
    lat = lax.axis_index("lat")
    lon = lax.axis_index("lon")
    has_up = lat < n_lat - 1
    has_dn = lat > 0
    right = lax.rem(lon + 1, n_lon)
    left = lax.rem(lon + n_lon - 1, n_lon)
    up_id = {"lon": lon, "lat": lat + 1}
    dn_id = {"lon": lon, "lat": lat - 1}
    right_id = {"lon": right, "lat": lat}
    left_id = {"lon": left, "lat": lat}

    half = n_lon // 2
    place = lax.rem(lon, half)
    far_right = place == half - 1
    far_left = place == 0
    is_far = far_right | far_left
    is_near = jnp.logical_not(is_far)
    far = jnp.where(far_right, right, left)
    partner = jnp.where(far_right, left, right)
    by_right_end = place == half - 2
    by_left_end = place == 1
    is_partner = by_right_end | by_left_end
    end = jnp.where(by_right_end, right, left)
    late_half = lon >= half
    early_half = jnp.logical_not(late_half)

    def field_copy(f):
        return pltpu.make_async_copy(flat_hbm.at[f], q_buf.at[f], own_sem.at[f])

    c_copy = pltpu.make_async_copy(c_flat_hbm, c_buf, own_sem.at[nf])
    small = [
        pltpu.make_async_copy(source, target, small_sem.at[i])
        for i, (source, target) in enumerate(
            [
                (cosz_hbm, cosz_ref),
                (albedo_hbm, albedo_ref),
                (ext_hbm, ext_ref),
                (ssa_hbm, ssa_ref),
                (weight_hbm, weight_ref),
                (order_hbm, order_ref),
                (count_hbm, count_ref),
            ]
        )
    ]

    barrier = pltpu.get_barrier_semaphore()

    def greet(device):
        pl.semaphore_signal(barrier, inc=1, device_id=device, device_id_type=MESH)

    @pl.when(is_far)
    def _():
        greet({"lon": partner, "lat": lat})
        greet({"lon": far, "lat": lat})

        @pl.when(has_up)
        def _():
            greet({"lon": partner, "lat": lat + 1})

        @pl.when(has_dn)
        def _():
            greet({"lon": partner, "lat": lat - 1})

    @pl.when(is_near)
    def _():
        @pl.when(has_up)
        def _():
            greet(up_id)

        @pl.when(has_dn)
        def _():
            greet(dn_id)

        @pl.when(jnp.logical_not(by_right_end))
        def _():
            greet(right_id)

        @pl.when(jnp.logical_not(by_left_end))
        def _():
            greet(left_id)

    for f in range(nf):
        field_copy(f).start()
    c_copy.start()
    for copy in small:
        copy.start()

    n_beside = has_up.astype(jnp.int32) + has_dn.astype(jnp.int32)

    @pl.when(is_near)
    def _():
        pl.semaphore_wait(barrier, 2 + n_beside + jnp.where(is_partner, n_beside, 0))

        @pl.when(is_partner)
        def _():
            pl.semaphore_signal(
                go_sem, inc=1, device_id={"lon": end, "lat": lat}, device_id_type=MESH
            )

    @pl.when(is_far)
    def _():
        pl.semaphore_wait(go_sem, 1)

    def z1_copy(f, side, r):
        if side == 0:
            source, target, device = rows - HALO + r, r, up_id
        else:
            source, target, device = r, HALO + r, dn_id
        return pltpu.make_async_remote_copy(
            src_ref=fields_hbm.at[f, :, source, 0],
            dst_ref=q_halo.at[f, target],
            send_sem=z1_send.at[side, f, r],
            recv_sem=z1_recv.at[side, f, r],
            device_id=device,
            device_id_type=MESH,
        )

    def z2_copy(f, side):
        if side == 0:
            source, target, device = rows, 0, up_id
        else:
            source, target, device = HALO, HALO + rows, dn_id
        return pltpu.make_async_remote_copy(
            src_ref=s_buf.at[f, pl.ds(source, HALO)],
            dst_ref=s_buf.at[f, pl.ds(target, HALO)],
            send_sem=z2_send.at[side, f],
            recv_sem=z2_recv.at[side, f],
            device_id=device,
            device_id_type=MESH,
        )

    cn_copy = pltpu.make_async_remote_copy(
        src_ref=courant_hbm.at[1, :, rows - 1, 0],
        dst_ref=c_north.at[0],
        send_sem=cn_send,
        recv_sem=cn_recv,
        device_id=up_id,
        device_id_type=MESH,
    )

    def x_copy(n, side):
        return pltpu.make_async_remote_copy(
            src_ref=pack_send.at[side, n],
            dst_ref=pack_recv.at[side, n],
            send_sem=x_send.at[side, n],
            recv_sem=x_recv.at[side, n],
            device_id=right_id if side == 0 else left_id,
            device_id_type=MESH,
        )

    @pl.when(has_up)
    def _():
        cn_copy.start()

    @pl.loop(0, nf)
    def _(f):
        @pl.when(has_up)
        def _():
            for r in range(HALO):
                z1_copy(f, 0, r).start()

        @pl.when(has_dn)
        def _():
            for r in range(HALO):
                z1_copy(f, 1, r).start()

    zero = jnp.zeros((8, lanes), jnp.float32)

    def fill_zero(ref):
        for g in range(groups):
            ref[pl.ds(8 * g, 8), :] = zero

    @pl.when(jnp.logical_not(has_dn))
    def _():
        fill_zero(c_north.at[0])

        @pl.loop(0, nf)
        def _(f):
            for r in range(HALO):
                fill_zero(q_halo.at[f, r])
                fill_zero(s_buf.at[f, r])

    @pl.when(jnp.logical_not(has_up))
    def _():
        @pl.loop(0, nf)
        def _(f):
            for r in range(HALO):
                fill_zero(q_halo.at[f, HALO + r])
                fill_zero(s_buf.at[f, HALO + rows + r])

    lane = lax.broadcasted_iota(jnp.int32, (8, lanes), 1)
    sub = lax.broadcasted_iota(jnp.int32, (8, lanes), 0)
    slot = lane >> 2
    own_half = (lane & 3) < 2
    low = sub < 4

    def pack(load):
        packed = zero
        for r in range(rows):
            for g in range(groups):
                k = r * groups + g
                packed = jnp.where(
                    slot == k, pltpu.roll(load(r, g), (4 * k + 2) % lanes, 1), packed
                )
        return packed

    def send_pair(n, even, odd):
        pack_send[0, n] = jnp.where(own_half, even, pltpu.roll(odd, 2, 1))
        pack_send[1, n] = jnp.where(own_half, pltpu.roll(even, lanes - 2, 1), odd)

    def recv_pair(n, odd):
        from_left = pack_recv[0, n]
        from_right = pack_recv[1, n]
        first = jnp.where(own_half, from_left, pltpu.roll(from_right, 2, 1))
        second = jnp.where(own_half, pltpu.roll(from_left, lanes - 2, 1), from_right)
        return jnp.where(odd, second, first)

    def own_row(f, r, g):
        return q_buf[f, pl.ds(8 * rows * g + r, 8, stride=rows), :]

    @pl.loop(0, nf)
    def _(f):
        field_copy(f).wait()
        pack_own[f] = pack(lambda r, g: own_row(f, r, g))

    c_copy.wait()
    pairs_f = nf // 2
    c_slot = 2 * pairs_f
    c_pack = pack(lambda r, g: c_buf[0, pl.ds(8 * rows * g + r, 8, stride=rows), :])
    for n in range(pairs_f):
        send_pair(n, pack_own[2 * n], pack_own[2 * n + 1])
    send_pair(c_slot, c_pack, c_pack)
    first_slots = list(range(pairs_f)) + [c_slot]

    def send_first(where, sides):
        for side in sides:
            @pl.when(where & jnp.logical_not(far_right if side == 0 else far_left))
            def _():
                for n in first_slots:
                    x_copy(n, side).start()

    def send_far(where):
        @pl.when(where & is_far)
        def _():
            pl.semaphore_wait(barrier, 1)

        for side in range(2):
            @pl.when(where & (far_right if side == 0 else far_left))
            def _():
                for n in first_slots:
                    x_copy(n, side).start()

    send_first(lon >= 0, (0, 1))
    send_far(late_half)

    for copy in small:
        copy.wait()
    cosz = jnp.concatenate([cosz_ref[...], cosz_ref[...]], axis=0)
    albedo = jnp.concatenate([albedo_ref[...], albedo_ref[...]], axis=0)
    neg_inv_mu = -1.0 / cosz
    ext = [
        jnp.where(low, ext_ref[2 * p], ext_ref[2 * p + 1]) * (4.0 / lev) for p in range(pairs)
    ]
    half_ssa = [jnp.where(low, ssa_ref[2 * p], ssa_ref[2 * p + 1]) * 0.5 for p in range(pairs)]
    weight = [jnp.where(low, weight_ref[2 * p], weight_ref[2 * p + 1]) for p in range(pairs)]

    ranks = lax.broadcasted_iota(jnp.int32, (lanes, lanes), 1)
    columns = lax.broadcasted_iota(jnp.int32, (lanes, lanes), 0)
    ones = jnp.ones((8, lanes), jnp.float32)
    sunlit = zero
    for r in range(rows):
        hit = (order_ref[r] == columns) & (ranks < count_ref[r])
        row = lax.dot_general(
            ones,
            hit.astype(jnp.float32),
            (((1,), (1,)), ((), ())),
            preferred_element_type=jnp.float32,
        )
        sunlit = jnp.where((sub & 3) == r, row, sunlit)
    sunlit = sunlit * float(lev)

    def optics(k, beam):
        raw = q_buf[1, pl.ds(pl.multiple_of(8 * k, 8), 8), :]
        water = jnp.maximum(raw, 0.0) + jnp.log1p(jnp.exp(-jnp.abs(raw)))
        turned = pltpu.roll(water, 4, 0)
        for half in range(2):
            level = 2 * k + half
            here = jnp.where(low, water, turned) if half == 0 else jnp.where(low, turned, water)
            after = []
            for p in range(pairs):
                tau = ext[p] * here
                direct = jnp.exp(tau * neg_inv_mu)
                decay = jnp.exp(tau * -1.66)
                rad_a[level, p] = decay
                rad_b[level, p] = half_ssa[p] * (beam[p] * (1.0 - direct))
                rad_g[level, p] = beam[p]
                after.append(beam[p] * direct)
            beam = tuple(after)
        return beam

    beam = lax.fori_loop(0, lev // 2, optics, tuple(cosz for _ in range(pairs)))

    def up_level(i, carry):
        level = lev - 1 - i
        a_below, b_below = carry
        a_out, b_out = [], []
        for p in range(pairs):
            decay = rad_a[level, p]
            source = rad_b[level, p]
            reflect = half_ssa[p] * (1.0 - decay)
            transmit = decay + reflect
            inv = 1.0 / (1.0 - reflect * a_below[p])
            through = transmit * inv
            a_here = reflect + transmit * through * a_below[p]
            b_here = through * (a_below[p] * source + b_below[p]) + source
            rad_a[level, p] = through
            rad_b[level, p] = (reflect * b_below[p] + source) * inv
            rad_c[level, p] = weight[p] * (1.0 - a_here)
            rad_g[level, p] = weight[p] * (rad_g[level, p] - b_here)
            a_out.append(a_here)
            b_out.append(b_here)
        return tuple(a_out), tuple(b_out)

    floor_b = tuple(albedo * beam[p] for p in range(pairs))
    for p in range(pairs):
        rad_c[lev, p] = weight[p] * (1.0 - albedo)
        rad_g[lev, p] = weight[p] * (beam[p] - floor_b[p])
    lax.fori_loop(0, lev, up_level, (tuple(albedo for _ in range(pairs)), floor_b))

    def net_flux(level, down):
        total = rad_c[level, 0] * down[0] + rad_g[level, 0]
        for p in range(1, pairs):
            total = total + (rad_c[level, p] * down[p] + rad_g[level, p])
        return total + pltpu.roll(total, 4, 0)

    def down_pair(k, carry):
        down, net = carry
        heats = []
        for half in range(2):
            level = 2 * k + half
            down = tuple(rad_a[level, p] * down[p] + rad_b[level, p] for p in range(pairs))
            below = net_flux(level + 1, down)
            heats.append((net - below) * sunlit)
            net = below
        heat_ref[pl.ds(pl.multiple_of(8 * k, 8), 8), :] = jnp.where(low, heats[0], heats[1])
        return down, net

    start = tuple(zero for _ in range(pairs))
    lax.fori_loop(0, lev // 2, down_pair, (start, net_flux(0, start)))
    send_far(early_half)

    def x_wait(n):
        x_copy(n, 0).wait_recv()
        x_copy(n, 1).wait_recv()

    x_wait(c_slot)

    @pl.when(has_dn)
    def _():
        cn_copy.wait_recv()

    c_halo = recv_pair(c_slot, False)
    for r in range(rows):
        for g in range(groups):
            k = r * groups + g
            here = c_buf[0, pl.ds(8 * rows * g + r, 8, stride=rows), :]
            edge = pltpu.roll(c_halo, (lanes - 2 - 4 * k) % lanes, 1)
            west = pltpu.roll(jnp.where(lane == lanes - 1, edge, here), 1, 1)
            c_west[r, pl.ds(8 * g, 8), :] = west * (1.0 / 12.0)
            c_east[r, pl.ds(8 * g, 8), :] = here * (1.0 / 12.0)
            north = c_buf[1, pl.ds(8 * rows * g + r, 8, stride=rows), :]
            c_north[r + 1, pl.ds(8 * g, 8), :] = north * (1.0 / 12.0)
    for g in range(groups):
        c_north[0, pl.ds(8 * g, 8), :] = c_north[0, pl.ds(8 * g, 8), :] * (1.0 / 12.0)

    first_lane = lane == 0
    first_two = lane < 2
    last_lane = lane == lanes - 1
    last_two = lane >= lanes - 2

    def tendency(load, halo, emit):
        for g in range(groups):
            at = pl.ds(8 * g, 8)
            q = [load(j, g, at) for j in range(rows + 2 * HALO)]
            north = [
                c_north[j, at, :] * (7.0 * (q[j + 1] + q[j + 2]) - (q[j] + q[j + 3]))
                for j in range(rows + 1)
            ]
            for r in range(rows):
                k = r * groups + g
                here = q[r + HALO]
                edge = pltpu.roll(halo, (lanes - 2 - 4 * k) % lanes, 1)
                r1 = pltpu.roll(jnp.where(first_lane, edge, here), lanes - 1, 1)
                r2 = pltpu.roll(jnp.where(first_two, edge, here), lanes - 2, 1)
                l1 = pltpu.roll(jnp.where(last_lane, edge, here), 1, 1)
                l2 = pltpu.roll(jnp.where(last_two, edge, here), 2, 1)
                east = c_east[r, at, :] * (7.0 * (here + r1) - (l1 + r2))
                west = c_west[r, at, :] * (7.0 * (l1 + here) - (l2 + r1))
                emit(r, g, here, -((east - west) + (north[r + 1] - north[r])))

    def z1_wait(f):
        @pl.when(has_dn)
        def _():
            for r in range(HALO):
                z1_copy(f, 0, r).wait_recv()

        @pl.when(has_up)
        def _():
            for r in range(HALO):
                z1_copy(f, 1, r).wait_recv()

    for n in range(pairs_f):
        x_wait(n)

    @pl.loop(0, pairs_f)
    def _(n):
        packed = []
        for odd in range(2):
            f = 2 * n + odd
            z1_wait(f)

            def emit(r, g, here, change):
                s_buf[f, HALO + r, pl.ds(8 * g, 8), :] = here + change

            def load(j, g, at):
                if j < HALO:
                    return q_halo[f, j, at, :]
                if j < HALO + rows:
                    return own_row(f, j - HALO, g)
                return q_halo[f, j - rows, at, :]

            tendency(load, recv_pair(n, odd == 1), emit)
            packed.append(pack(lambda r, g: s_buf[f, HALO + r, pl.ds(8 * g, 8), :]))

            @pl.when(has_up)
            def _():
                z2_copy(f, 0).start()

            @pl.when(has_dn)
            def _():
                z2_copy(f, 1).start()

        m = pairs_f + n
        send_pair(m, packed[0], packed[1])
        x_copy(m, 0).start()
        x_copy(m, 1).start()

    def final(f, halo, extra):
        def emit(r, g, here, change):
            value = 0.5 * ((own_row(f, r, g) + here) + change)
            if extra:
                value = value + 0.5 * heat_ref[pl.ds(8 * rows * g + r, 8, stride=rows), :]
            out_ref[f, pl.ds(8 * rows * g + r, 8, stride=rows), :] = value

        @pl.when(has_dn)
        def _():
            z2_copy(f, 0).wait_recv()

        @pl.when(has_up)
        def _():
            z2_copy(f, 1).wait_recv()

        tendency(lambda j, g, at: s_buf[f, j, at, :], halo, emit)

    x_wait(pairs_f)
    final(0, recv_pair(pairs_f, False), True)

    @pl.loop(1, nf)
    def _(f):
        n = pairs_f + f // 2

        @pl.when(f % 2 == 0)
        def _():
            x_wait(n)

        final(f, recv_pair(n, f % 2 == 1), False)

    @pl.loop(0, nf)
    def _(f):
        @pl.when(has_up)
        def _():
            for r in range(HALO):
                z1_copy(f, 0, r).wait_send()
            z2_copy(f, 0).wait_send()

        @pl.when(has_dn)
        def _():
            for r in range(HALO):
                z1_copy(f, 1, r).wait_send()
            z2_copy(f, 1).wait_send()

    @pl.when(has_up)
    def _():
        cn_copy.wait_send()

    for n in range(2 * pairs_f + 1):
        x_copy(n, 0).wait_send()
        x_copy(n, 1).wait_send()


def store_kernel(parts, new_ref, heat_ref, new_hbm, out_heat_hbm, sem):
    copies = [
        pltpu.make_async_copy(new_ref.at[f], new_hbm.at[f], sem.at[f]) for f in range(parts)
    ]
    copies.append(pltpu.make_async_copy(heat_ref, out_heat_hbm, sem.at[parts]))
    for copy in copies:
        copy.start()
    for copy in copies:
        copy.wait()


def per_device(n_lat, n_lon, fields, courant, cosz, albedo, ext, ssa, weight, order, count):
    nf, lev, rows, lanes = fields.shape
    bands = ext.shape[0]
    dims = (nf, lev, rows, lanes, bands, n_lat, n_lon)
    tall = rows + 2 * HALO
    f32 = jnp.float32
    hbm_spec = pl.BlockSpec(memory_space=pltpu.HBM)
    vmem_spec = pl.BlockSpec(memory_space=pltpu.VMEM)
    rad = pltpu.VMEM((lev + 1, bands // 2, 8, lanes), f32)
    packs = nf + 1
    results = (
        jax.ShapeDtypeStruct((nf, lev * rows, lanes), f32),
        jax.ShapeDtypeStruct((lev * rows, lanes), f32),
    )
    out, heat = pl.pallas_call(
        functools.partial(step_kernel, dims),
        out_shape=(
            pltpu.VMEM((nf, lev * rows, lanes), f32),
            pltpu.VMEM((lev * rows, lanes), f32),
        ),
        in_specs=[hbm_spec] * 11,
        out_specs=(vmem_spec, vmem_spec),
        scratch_shapes=[
            pltpu.VMEM((nf, lev * rows, lanes), f32),
            pltpu.VMEM((nf, 2 * HALO, lev, lanes), f32),
            pltpu.VMEM((nf, tall, lev, lanes), f32),
            pltpu.VMEM((2, lev * rows, lanes), f32),
            pltpu.VMEM((rows, lev, lanes), f32),
            pltpu.VMEM((rows, lev, lanes), f32),
            pltpu.VMEM((rows + 1, lev, lanes), f32),
            pltpu.VMEM((rows, lanes), f32),
            pltpu.VMEM((rows, lanes), f32),
            pltpu.SMEM((bands,), f32),
            pltpu.SMEM((bands,), f32),
            pltpu.SMEM((bands,), f32),
            pltpu.VMEM((rows, 1, lanes), jnp.int32),
            pltpu.SMEM((rows,), jnp.int32),
            rad,
            rad,
            rad,
            rad,
            pltpu.VMEM((nf, 8, lanes), f32),
            pltpu.VMEM((2, packs, 8, lanes), f32),
            pltpu.VMEM((2, packs, 8, lanes), f32),
            pltpu.SemaphoreType.DMA((nf + 1,)),
            pltpu.SemaphoreType.DMA((7,)),
            pltpu.SemaphoreType.REGULAR,
            pltpu.SemaphoreType.DMA((2, nf, HALO)),
            pltpu.SemaphoreType.DMA((2, nf, HALO)),
            pltpu.SemaphoreType.DMA((2, nf)),
            pltpu.SemaphoreType.DMA((2, nf)),
            pltpu.SemaphoreType.DMA,
            pltpu.SemaphoreType.DMA,
            pltpu.SemaphoreType.DMA((2, packs)),
            pltpu.SemaphoreType.DMA((2, packs)),
        ],
        compiler_params=pltpu.CompilerParams(
            collective_id=0, has_side_effects=True, vmem_limit_bytes=48 * 1024 * 1024
        ),
        name="advect_radiate",
    )(
        *(
            pltpu.with_memory_space_constraint(x, pltpu.HBM)
            for x in (
                fields.reshape(nf, lev, rows, 1, lanes),
                fields.reshape(nf, lev * rows, lanes),
                courant.reshape(2, lev, rows, 1, lanes),
                courant.reshape(2, lev * rows, lanes),
                cosz,
                albedo,
                ext,
                ssa,
                weight,
                order,
                count.reshape(rows),
            )
        )
    )
    out, heat = pl.pallas_call(
        functools.partial(store_kernel, nf),
        out_shape=results,
        in_specs=[pl.BlockSpec(memory_space=pl.ANY)] * 2,
        out_specs=(hbm_spec, hbm_spec),
        scratch_shapes=[pltpu.SemaphoreType.DMA((nf + 1,))],
        compiler_params=pltpu.CompilerParams(vmem_limit_bytes=32 * 1024 * 1024),
        name="store_results",
    )(out, heat)
    return out.reshape(nf, lev, rows, lanes), heat.reshape(lev, rows, lanes)


def solution(mesh):
    n_lat, n_lon = mesh.shape["lat"], mesh.shape["lon"]
    in_specs = (
        P(None, None, "lat", "lon"),
        P(None, None, "lat", "lon"),
        P("lat", "lon"),
        P("lat", "lon"),
        P(),
        P(),
        P(),
        P("lat", "lon", None),
        P("lat", "lon"),
    )
    out_specs = (P(None, None, "lat", "lon"), P(None, "lat", "lon"))
    return jax.shard_map(
        functools.partial(per_device, n_lat, n_lon),
        mesh=mesh,
        in_specs=in_specs,
        out_specs=out_specs,
        check_vma=False,
    )
```

```python
import functools

import jax
import jax.numpy as jnp
from jax import lax
from jax.experimental import pallas as pl
from jax.experimental.pallas import tpu as pltpu
from jax.sharding import PartitionSpec as P

MESH = pl.DeviceIdType.MESH
HALO = 2
EARLY = 4


def step_kernel(
    dims,
    fields_hbm,
    flat_hbm,
    courant_hbm,
    c_flat_hbm,
    cosz_hbm,
    albedo_hbm,
    ext_hbm,
    ssa_hbm,
    weight_hbm,
    order_hbm,
    count_hbm,
    out_ref,
    heat_ref,
    q_buf,
    q_halo,
    s_buf,
    c_buf,
    c_east,
    c_west,
    c_north,
    cosz_ref,
    albedo_ref,
    ext_ref,
    ssa_ref,
    weight_ref,
    order_ref,
    count_ref,
    rad_a,
    rad_b,
    rad_c,
    rad_g,
    band,
    c_edge,
    pack_q,
    pack_s,
    edge_buf,
    send_1,
    recv_1,
    send_2,
    recv_2,
    own_sem,
    small_sem,
    go_sem,
    z1_send,
    z1_recv,
    z2_send,
    z2_recv,
    cn_send,
    cn_recv,
    x1_send,
    x1_recv,
    x2_send,
    x2_recv,
):
    nf, lev, rows, lanes, bands, n_lat, n_lon = dims
    groups = lev // 8
    pairs = bands // 2
    lat = lax.axis_index("lat")
    lon = lax.axis_index("lon")
    has_up = lat < n_lat - 1
    has_dn = lat > 0
    right = lax.rem(lon + 1, n_lon)
    left = lax.rem(lon + n_lon - 1, n_lon)
    up_id = {"lon": lon, "lat": lat + 1}
    dn_id = {"lon": lon, "lat": lat - 1}
    right_id = {"lon": right, "lat": lat}
    left_id = {"lon": left, "lat": lat}

    half = n_lon // 2
    place = lax.rem(lon, half)
    far_right = place == half - 1
    far_left = place == 0
    is_far = far_right | far_left
    is_near = jnp.logical_not(is_far)
    far = jnp.where(far_right, right, left)
    partner = jnp.where(far_right, left, right)
    by_right_end = place == half - 2
    by_left_end = place == 1
    is_partner = by_right_end | by_left_end
    end = jnp.where(by_right_end, right, left)
    late_half = lon >= half
    early_half = jnp.logical_not(late_half)

    def field_copy(f):
        return pltpu.make_async_copy(flat_hbm.at[f], q_buf.at[f], own_sem.at[f])

    c_copy = pltpu.make_async_copy(c_flat_hbm, c_buf, own_sem.at[nf])
    small = [
        pltpu.make_async_copy(source, target, small_sem.at[i])
        for i, (source, target) in enumerate(
            [
                (cosz_hbm, cosz_ref),
                (albedo_hbm, albedo_ref),
                (ext_hbm, ext_ref),
                (ssa_hbm, ssa_ref),
                (weight_hbm, weight_ref),
                (order_hbm, order_ref),
                (count_hbm, count_ref),
            ]
        )
    ]

    barrier = pltpu.get_barrier_semaphore()

    def greet(device):
        pl.semaphore_signal(barrier, inc=1, device_id=device, device_id_type=MESH)

    @pl.when(is_far)
    def _():
        greet({"lon": partner, "lat": lat})
        greet({"lon": far, "lat": lat})

        @pl.when(has_up)
        def _():
            greet({"lon": partner, "lat": lat + 1})

        @pl.when(has_dn)
        def _():
            greet({"lon": partner, "lat": lat - 1})

    @pl.when(is_near)
    def _():
        @pl.when(has_up)
        def _():
            greet(up_id)

        @pl.when(has_dn)
        def _():
            greet(dn_id)

        @pl.when(jnp.logical_not(by_right_end))
        def _():
            greet(right_id)

        @pl.when(jnp.logical_not(by_left_end))
        def _():
            greet(left_id)

    for f in range(nf):
        field_copy(f).start()
    c_copy.start()
    for copy in small:
        copy.start()

    n_beside = has_up.astype(jnp.int32) + has_dn.astype(jnp.int32)

    @pl.when(is_near)
    def _():
        pl.semaphore_wait(barrier, 2 + n_beside + jnp.where(is_partner, n_beside, 0))

        @pl.when(is_partner)
        def _():
            pl.semaphore_signal(
                go_sem, inc=1, device_id={"lon": end, "lat": lat}, device_id_type=MESH
            )

    @pl.when(is_far)
    def _():
        pl.semaphore_wait(go_sem, 1)

    def z1_copy(f, side, r):
        if side == 0:
            source, target, device = rows - HALO + r, r, up_id
        else:
            source, target, device = r, HALO + r, dn_id
        return pltpu.make_async_remote_copy(
            src_ref=fields_hbm.at[f, :, source, 0],
            dst_ref=q_halo.at[f, target],
            send_sem=z1_send.at[side, f, r],
            recv_sem=z1_recv.at[side, f, r],
            device_id=device,
            device_id_type=MESH,
        )

    def z2_copy(f, side):
        if side == 0:
            source, target, device = rows, 0, up_id
        else:
            source, target, device = HALO, HALO + rows, dn_id
        return pltpu.make_async_remote_copy(
            src_ref=s_buf.at[f, pl.ds(source, HALO)],
            dst_ref=s_buf.at[f, pl.ds(target, HALO)],
            send_sem=z2_send.at[side, f],
            recv_sem=z2_recv.at[side, f],
            device_id=device,
            device_id_type=MESH,
        )

    cn_copy = pltpu.make_async_remote_copy(
        src_ref=courant_hbm.at[1, :, rows - 1, 0],
        dst_ref=c_north.at[0],
        send_sem=cn_send,
        recv_sem=cn_recv,
        device_id=up_id,
        device_id_type=MESH,
    )

    def x1_copy(side):
        return pltpu.make_async_remote_copy(
            src_ref=send_1.at[side],
            dst_ref=recv_1.at[side],
            send_sem=x1_send.at[side],
            recv_sem=x1_recv.at[side],
            device_id=right_id if side == 0 else left_id,
            device_id_type=MESH,
        )

    def x2_copy(n, side):
        return pltpu.make_async_remote_copy(
            src_ref=send_2.at[side, n],
            dst_ref=recv_2.at[side, n],
            send_sem=x2_send.at[side, n],
            recv_sem=x2_recv.at[side, n],
            device_id=right_id if side == 0 else left_id,
            device_id_type=MESH,
        )

    @pl.when(has_up)
    def _():
        cn_copy.start()

    def z1_start(f):
        @pl.when(has_up)
        def _():
            for r in range(HALO):
                z1_copy(f, 0, r).start()

        @pl.when(has_dn)
        def _():
            for r in range(HALO):
                z1_copy(f, 1, r).start()

    pl.loop(0, EARLY)(z1_start)

    @pl.when(is_near)
    def _():
        pl.loop(EARLY, nf)(z1_start)

    zero = jnp.zeros((8, lanes), jnp.float32)

    def fill_zero(ref):
        for g in range(groups):
            ref[pl.ds(8 * g, 8), :] = zero

    @pl.when(jnp.logical_not(has_dn))
    def _():
        fill_zero(c_north.at[0])

        @pl.loop(0, nf)
        def _(f):
            for r in range(HALO):
                fill_zero(q_halo.at[f, r])
                fill_zero(s_buf.at[f, r])

    @pl.when(jnp.logical_not(has_up))
    def _():
        @pl.loop(0, nf)
        def _(f):
            for r in range(HALO):
                fill_zero(q_halo.at[f, HALO + r])
                fill_zero(s_buf.at[f, HALO + rows + r])

    lane = lax.broadcasted_iota(jnp.int32, (8, lanes), 1)
    sub = lax.broadcasted_iota(jnp.int32, (8, lanes), 0)
    slot = lane >> 2
    own_half = (lane & 3) < 2
    low = sub < 4

    def pack(load):
        packed = zero
        for r in range(rows):
            for g in range(groups):
                k = r * groups + g
                packed = jnp.where(
                    slot == k, pltpu.roll(load(r, g), (4 * k + 2) % lanes, 1), packed
                )
        return packed

    def send_pair(buf, n, even, odd):
        buf[0, n] = jnp.where(own_half, even, pltpu.roll(odd, 2, 1))
        buf[1, n] = jnp.where(own_half, pltpu.roll(even, lanes - 2, 1), odd)

    def recv_pair(buf, n, odd):
        from_left = buf[0, n]
        from_right = buf[1, n]
        first = jnp.where(own_half, from_left, pltpu.roll(from_right, 2, 1))
        second = jnp.where(own_half, pltpu.roll(from_left, lanes - 2, 1), from_right)
        return jnp.where(odd, second, first)

    def own_row(f, r, g):
        return q_buf[f, pl.ds(8 * rows * g + r, 8, stride=rows), :]

    def courant_row(n, r, g):
        return c_buf[n, pl.ds(8 * rows * g + r, 8, stride=rows), :]

    @pl.loop(0, nf)
    def _(f):
        field_copy(f).wait()
        pack_q[f] = pack(lambda r, g: own_row(f, r, g))

    c_copy.wait()
    pairs_f = nf // 2
    c_pack = pack(lambda r, g: courant_row(0, r, g))
    for n in range(pairs_f):
        send_pair(send_1, n, pack_q[2 * n], pack_q[2 * n + 1])
    send_pair(send_1, pairs_f, c_pack, c_pack)
    c_edge[0] = c_pack * (1.0 / 12.0)

    for side in range(2):
        @pl.when(jnp.logical_not(far_right if side == 0 else far_left))
        def _():
            x1_copy(side).start()

    def send_far(where):
        @pl.when(where & is_far)
        def _():
            pl.semaphore_wait(barrier, 1)

        for side in range(2):
            @pl.when(where & (far_right if side == 0 else far_left))
            def _():
                x1_copy(side).start()

        @pl.when(where & is_far)
        def _():
            pl.loop(EARLY, nf)(z1_start)

    send_far(late_half)

    ahead = lax.broadcasted_iota(jnp.int32, (2 * lanes, 2 * lanes), 0) & (lanes - 1)
    column = lax.broadcasted_iota(jnp.int32, (2 * lanes, 2 * lanes), 1)
    ahead = ahead - jnp.where(column < lanes, column, column - lanes - 1)
    inner = (ahead == 0) | (ahead == 1)
    outer = (ahead == -1) | (ahead == 2)
    band[...] = jnp.where(inner, 7.0, jnp.where(outer, -1.0, 0.0)).astype(jnp.bfloat16)

    for copy in small:
        copy.wait()
    cosz = jnp.concatenate([cosz_ref[...], cosz_ref[...]], axis=0)
    albedo = jnp.concatenate([albedo_ref[...], albedo_ref[...]], axis=0)
    neg_inv_mu = -1.0 / cosz
    ext = [
        jnp.where(low, ext_ref[2 * p], ext_ref[2 * p + 1]) * (4.0 / lev) for p in range(pairs)
    ]
    half_ssa = [jnp.where(low, ssa_ref[2 * p], ssa_ref[2 * p + 1]) * 0.5 for p in range(pairs)]
    weight = [jnp.where(low, weight_ref[2 * p], weight_ref[2 * p + 1]) for p in range(pairs)]

    ranks = lax.broadcasted_iota(jnp.int32, (lanes, lanes), 1)
    columns = lax.broadcasted_iota(jnp.int32, (lanes, lanes), 0)
    ones = jnp.ones((8, lanes), jnp.float32)
    sunlit = zero
    for r in range(rows):
        hit = (order_ref[r] == columns) & (ranks < count_ref[r])
        row = lax.dot_general(
            ones,
            hit.astype(jnp.float32),
            (((1,), (1,)), ((), ())),
            preferred_element_type=jnp.float32,
        )
        sunlit = jnp.where((sub & 3) == r, row, sunlit)
    sunlit = sunlit * float(lev)

    def optics(k, beam):
        raw = q_buf[1, pl.ds(pl.multiple_of(8 * k, 8), 8), :]
        water = jnp.maximum(raw, 0.0) + jnp.log1p(jnp.exp(-jnp.abs(raw)))
        turned = pltpu.roll(water, 4, 0)
        for half in range(2):
            level = 2 * k + half
            here = jnp.where(low, water, turned) if half == 0 else jnp.where(low, turned, water)
            after = []
            for p in range(pairs):
                tau = ext[p] * here
                direct = jnp.exp(tau * neg_inv_mu)
                decay = jnp.exp(tau * -1.66)
                rad_a[level, p] = decay
                rad_b[level, p] = half_ssa[p] * (beam[p] * (1.0 - direct))
                rad_g[level, p] = beam[p]
                after.append(beam[p] * direct)
            beam = tuple(after)
        return beam

    beam = lax.fori_loop(0, lev // 2, optics, tuple(cosz for _ in range(pairs)))

    def up_level(i, carry):
        level = lev - 1 - i
        a_below, b_below = carry
        a_out, b_out = [], []
        for p in range(pairs):
            decay = rad_a[level, p]
            source = rad_b[level, p]
            reflect = half_ssa[p] * (1.0 - decay)
            transmit = decay + reflect
            inv = 1.0 / (1.0 - reflect * a_below[p])
            through = transmit * inv
            a_here = reflect + transmit * through * a_below[p]
            b_here = through * (a_below[p] * source + b_below[p]) + source
            rad_a[level, p] = through
            rad_b[level, p] = (reflect * b_below[p] + source) * inv
            rad_c[level, p] = weight[p] * (1.0 - a_here)
            rad_g[level, p] = weight[p] * (rad_g[level, p] - b_here)
            a_out.append(a_here)
            b_out.append(b_here)
        return tuple(a_out), tuple(b_out)

    floor_b = tuple(albedo * beam[p] for p in range(pairs))
    for p in range(pairs):
        rad_c[lev, p] = weight[p] * (1.0 - albedo)
        rad_g[lev, p] = weight[p] * (beam[p] - floor_b[p])
    lax.fori_loop(0, lev, up_level, (tuple(albedo for _ in range(pairs)), floor_b))

    def net_flux(level, down):
        total = rad_c[level, 0] * down[0] + rad_g[level, 0]
        for p in range(1, pairs):
            total = total + (rad_c[level, p] * down[p] + rad_g[level, p])
        return total + pltpu.roll(total, 4, 0)

    def down_pair(k, carry):
        down, net = carry
        heats = []
        for half in range(2):
            level = 2 * k + half
            down = tuple(rad_a[level, p] * down[p] + rad_b[level, p] for p in range(pairs))
            below = net_flux(level + 1, down)
            heats.append((net - below) * sunlit)
            net = below
        heat_ref[pl.ds(pl.multiple_of(8 * k, 8), 8), :] = jnp.where(low, heats[0], heats[1])
        return down, net

    start = tuple(zero for _ in range(pairs))
    lax.fori_loop(0, lev // 2, down_pair, (start, net_flux(0, start)))
    send_far(early_half)

    @pl.when(has_dn)
    def _():
        cn_copy.wait_recv()

    for r in range(rows):
        for g in range(groups):
            here = courant_row(0, r, g) * (1.0 / 12.0)
            c_east[r, pl.ds(8 * g, 8), :] = here
            c_west[r, pl.ds(8 * g, 8), :] = jnp.where(lane == 0, 0.0, pltpu.roll(here, 1, 1))
            c_north[r + 1, pl.ds(8 * g, 8), :] = courant_row(1, r, g) * (1.0 / 12.0)
    for g in range(groups):
        c_north[0, pl.ds(8 * g, 8), :] = c_north[0, pl.ds(8 * g, 8), :] * (1.0 / 12.0)

    def tendency(load, emit):
        x = jnp.concatenate(
            [load(HALO + r, g) for r in range(rows) for g in range(groups)], axis=0
        )
        upper = x.astype(jnp.bfloat16)
        lower = (x - upper.astype(jnp.float32)).astype(jnp.bfloat16)
        flux = jnp.dot(
            jnp.concatenate([upper, lower], axis=1),
            band[...],
            preferred_element_type=jnp.float32,
        )
        for g in range(groups):
            at = pl.ds(8 * g, 8)
            q = [load(j, g) for j in range(rows + 2 * HALO)]
            north = [
                c_north[j, at, :] * (7.0 * (q[j + 1] + q[j + 2]) - (q[j] + q[j + 3]))
                for j in range(rows + 1)
            ]
            for r in range(rows):
                k = r * groups + g
                east = c_east[r, at, :] * flux[8 * k : 8 * k + 8, :lanes]
                west = c_west[r, at, :] * flux[8 * k : 8 * k + 8, lanes:]
                emit(r, g, q[r + HALO], (north[r] - north[r + 1]) - (east - west))

    corner = lane & 3

    def edge(halo, own):
        m1 = pltpu.roll(halo, 1, 1)
        m2 = pltpu.roll(halo, 2, 1)
        p1 = pltpu.roll(halo, lanes - 1, 1)
        p2 = pltpu.roll(halo, lanes - 2, 1)
        beside = pltpu.roll(own, lanes - 1, 1)
        east = jnp.where(
            corner == 0,
            -p2,
            jnp.where(corner == 1, 7.0 * p1 - p2, jnp.where(corner == 2, -m1, 0.0)),
        )
        west = jnp.where(
            corner == 0,
            0.0,
            jnp.where(
                corner == 1,
                -p1,
                jnp.where(corner == 2, 7.0 * (m1 + own) - (m2 + beside), -m2),
            ),
        )
        return c_edge[1] * west - c_edge[0] * east

    edge_lanes = (lane < 2) | (lane >= lanes - 2)

    def spread(packed, k):
        return jnp.where(edge_lanes, pltpu.roll(packed, (lanes - 2 - 4 * k) % lanes, 1), 0.0)

    def x1_wait():
        x1_copy(0).wait_recv()
        x1_copy(1).wait_recv()
        beyond = recv_pair(recv_1, pairs_f, False) * (1.0 / 12.0)
        c_edge[1] = jnp.where(
            corner == 2, pltpu.roll(beyond, 1, 1), pltpu.roll(c_edge[0], 1, 1)
        )

    def z1_wait(f):
        @pl.when(has_dn)
        def _():
            for r in range(HALO):
                z1_copy(f, 0, r).wait_recv()

        @pl.when(has_up)
        def _():
            for r in range(HALO):
                z1_copy(f, 1, r).wait_recv()

    def add_edge(f):
        change = edge(recv_pair(recv_1, f // 2, f % 2 == 1), pack_q[f])
        edge_buf[f] = change
        pack_s[f] = pack_s[f] + change

        @pl.when(f % 2 == 1)
        def _():
            n = f // 2
            send_pair(send_2, n, pack_s[f - 1], pack_s[f])
            x2_copy(n, 0).start()
            x2_copy(n, 1).start()

    def finish_section(f):
        change = edge_buf[f]
        for r in range(rows):
            for g in range(groups):
                at = pl.ds(8 * g, 8)
                s_buf[f, HALO + r, at, :] = s_buf[f, HALO + r, at, :] + spread(
                    change, r * groups + g
                )

        @pl.when(has_up)
        def _():
            z2_copy(f, 0).start()

        @pl.when(has_dn)
        def _():
            z2_copy(f, 1).start()

    pl.when(is_near)(x1_wait)

    @pl.loop(0, nf)
    def _(f):
        z1_wait(f)

        def load(j, g):
            at = pl.ds(8 * g, 8)
            if j < HALO:
                return q_halo[f, j, at, :]
            if j < HALO + rows:
                return own_row(f, j - HALO, g)
            return q_halo[f, j - rows, at, :]

        parts = [zero] * rows

        def emit(r, g, here, change):
            k = r * groups + g
            value = here + change
            s_buf[f, HALO + r, pl.ds(8 * g, 8), :] = value
            parts[r] = jnp.where(slot == k, pltpu.roll(value, (4 * k + 2) % lanes, 1), parts[r])

        tendency(load, emit)
        pack_s[f] = sum(parts[1:], parts[0])

        @pl.when(is_near)
        def _():
            add_edge(f)
            finish_section(f)

    @pl.when(is_far)
    def _():
        x1_wait()
        pl.loop(0, nf)(add_edge)
        pl.loop(0, nf)(finish_section)

    @pl.loop(0, nf)
    def _(f):
        n = f // 2

        @pl.when(f % 2 == 0)
        def _():
            x2_copy(n, 0).wait_recv()
            x2_copy(n, 1).wait_recv()

        @pl.when(has_dn)
        def _():
            z2_copy(f, 0).wait_recv()

        @pl.when(has_up)
        def _():
            z2_copy(f, 1).wait_recv()

        beyond = edge(recv_pair(recv_2, n, f % 2 == 1), pack_s[f])

        def emit(r, g, here, change):
            total = (own_row(f, r, g) + here) + (change + spread(beyond, r * groups + g))
            out_ref[f, pl.ds(8 * rows * g + r, 8, stride=rows), :] = 0.5 * total

        tendency(lambda j, g: s_buf[f, j, pl.ds(8 * g, 8), :], emit)

        @pl.when(f == 0)
        def _():
            for i in range(rows * groups):
                at = pl.ds(8 * i, 8)
                out_ref[0, at, :] = out_ref[0, at, :] + 0.5 * heat_ref[at, :]

    @pl.loop(0, nf)
    def _(f):
        @pl.when(has_up)
        def _():
            for r in range(HALO):
                z1_copy(f, 0, r).wait_send()
            z2_copy(f, 0).wait_send()

        @pl.when(has_dn)
        def _():
            for r in range(HALO):
                z1_copy(f, 1, r).wait_send()
            z2_copy(f, 1).wait_send()

    @pl.when(has_up)
    def _():
        cn_copy.wait_send()

    for side in range(2):
        x1_copy(side).wait_send()
        for n in range(pairs_f):
            x2_copy(n, side).wait_send()


def store_kernel(parts, new_ref, heat_ref, new_hbm, out_heat_hbm, sem):
    copies = [
        pltpu.make_async_copy(new_ref.at[f], new_hbm.at[f], sem.at[f]) for f in range(parts)
    ]
    copies.append(pltpu.make_async_copy(heat_ref, out_heat_hbm, sem.at[parts]))
    for copy in copies:
        copy.start()
    for copy in copies:
        copy.wait()


def per_device(n_lat, n_lon, fields, courant, cosz, albedo, ext, ssa, weight, order, count):
    nf, lev, rows, lanes = fields.shape
    bands = ext.shape[0]
    dims = (nf, lev, rows, lanes, bands, n_lat, n_lon)
    tall = rows + 2 * HALO
    f32 = jnp.float32
    hbm_spec = pl.BlockSpec(memory_space=pltpu.HBM)
    vmem_spec = pl.BlockSpec(memory_space=pltpu.VMEM)
    rad = pltpu.VMEM((lev + 1, bands // 2, 8, lanes), f32)
    pairs_f = nf // 2
    results = (
        jax.ShapeDtypeStruct((nf, lev * rows, lanes), f32),
        jax.ShapeDtypeStruct((lev * rows, lanes), f32),
    )
    out, heat = pl.pallas_call(
        functools.partial(step_kernel, dims),
        out_shape=(
            pltpu.VMEM((nf, lev * rows, lanes), f32),
            pltpu.VMEM((lev * rows, lanes), f32),
        ),
        in_specs=[hbm_spec] * 11,
        out_specs=(vmem_spec, vmem_spec),
        scratch_shapes=[
            pltpu.VMEM((nf, lev * rows, lanes), f32),
            pltpu.VMEM((nf, 2 * HALO, lev, lanes), f32),
            pltpu.VMEM((nf, tall, lev, lanes), f32),
            pltpu.VMEM((2, lev * rows, lanes), f32),
            pltpu.VMEM((rows, lev, lanes), f32),
            pltpu.VMEM((rows, lev, lanes), f32),
            pltpu.VMEM((rows + 1, lev, lanes), f32),
            pltpu.VMEM((rows, lanes), f32),
            pltpu.VMEM((rows, lanes), f32),
            pltpu.SMEM((bands,), f32),
            pltpu.SMEM((bands,), f32),
            pltpu.SMEM((bands,), f32),
            pltpu.VMEM((rows, 1, lanes), jnp.int32),
            pltpu.SMEM((rows,), jnp.int32),
            rad,
            rad,
            rad,
            rad,
            pltpu.VMEM((2 * lanes, 2 * lanes), jnp.bfloat16),
            pltpu.VMEM((2, 8, lanes), f32),
            pltpu.VMEM((nf, 8, lanes), f32),
            pltpu.VMEM((nf, 8, lanes), f32),
            pltpu.VMEM((nf, 8, lanes), f32),
            pltpu.VMEM((2, pairs_f + 1, 8, lanes), f32),
            pltpu.VMEM((2, pairs_f + 1, 8, lanes), f32),
            pltpu.VMEM((2, pairs_f, 8, lanes), f32),
            pltpu.VMEM((2, pairs_f, 8, lanes), f32),
            pltpu.SemaphoreType.DMA((nf + 1,)),
            pltpu.SemaphoreType.DMA((7,)),
            pltpu.SemaphoreType.REGULAR,
            pltpu.SemaphoreType.DMA((2, nf, HALO)),
            pltpu.SemaphoreType.DMA((2, nf, HALO)),
            pltpu.SemaphoreType.DMA((2, nf)),
            pltpu.SemaphoreType.DMA((2, nf)),
            pltpu.SemaphoreType.DMA,
            pltpu.SemaphoreType.DMA,
            pltpu.SemaphoreType.DMA((2,)),
            pltpu.SemaphoreType.DMA((2,)),
            pltpu.SemaphoreType.DMA((2, pairs_f)),
            pltpu.SemaphoreType.DMA((2, pairs_f)),
        ],
        compiler_params=pltpu.CompilerParams(
            collective_id=0, has_side_effects=True, vmem_limit_bytes=48 * 1024 * 1024
        ),
        name="advect_radiate",
    )(
        *(
            pltpu.with_memory_space_constraint(x, pltpu.HBM)
            for x in (
                fields.reshape(nf, lev, rows, 1, lanes),
                fields.reshape(nf, lev * rows, lanes),
                courant.reshape(2, lev, rows, 1, lanes),
                courant.reshape(2, lev * rows, lanes),
                cosz,
                albedo,
                ext,
                ssa,
                weight,
                order,
                count.reshape(rows),
            )
        )
    )
    out, heat = pl.pallas_call(
        functools.partial(store_kernel, nf),
        out_shape=results,
        in_specs=[pl.BlockSpec(memory_space=pl.ANY)] * 2,
        out_specs=(hbm_spec, hbm_spec),
        scratch_shapes=[pltpu.SemaphoreType.DMA((nf + 1,))],
        compiler_params=pltpu.CompilerParams(vmem_limit_bytes=32 * 1024 * 1024),
        name="store_results",
    )(out, heat)
    return out.reshape(nf, lev, rows, lanes), heat.reshape(lev, rows, lanes)


def solution(mesh):
    n_lat, n_lon = mesh.shape["lat"], mesh.shape["lon"]
    in_specs = (
        P(None, None, "lat", "lon"),
        P(None, None, "lat", "lon"),
        P("lat", "lon"),
        P("lat", "lon"),
        P(),
        P(),
        P(),
        P("lat", "lon", None),
        P("lat", "lon"),
    )
    out_specs = (P(None, None, "lat", "lon"), P(None, "lat", "lon"))
    return jax.shard_map(
        functools.partial(per_device, n_lat, n_lon),
        mesh=mesh,
        in_specs=in_specs,
        out_specs=out_specs,
        check_vma=False,
    )
```

```python
import functools

import jax
import jax.numpy as jnp
from jax import lax
from jax.experimental import pallas as pl
from jax.experimental.pallas import tpu as pltpu
from jax.sharding import PartitionSpec as P

MESH = pl.DeviceIdType.MESH
HALO = 2
EARLY_FIRST = 4
EARLY_SECOND = 2


def step_kernel(
    dims,
    fields_hbm,
    flat_hbm,
    courant_hbm,
    c_flat_hbm,
    cosz_hbm,
    albedo_hbm,
    ext_hbm,
    ssa_hbm,
    weight_hbm,
    order_hbm,
    count_hbm,
    out_ref,
    heat_ref,
    q_buf,
    q_halo,
    s_buf,
    c_buf,
    c_east,
    c_west,
    c_north,
    cosz_ref,
    albedo_ref,
    ext_ref,
    ssa_ref,
    weight_ref,
    order_ref,
    count_ref,
    rad_a,
    rad_b,
    rad_c,
    rad_g,
    band,
    c_edge,
    pack_q,
    pack_s,
    edge_buf,
    send_1,
    recv_1,
    send_2,
    recv_2,
    own_sem,
    small_sem,
    go_sem,
    z1_send,
    z1_recv,
    z2_send,
    z2_recv,
    cn_send,
    cn_recv,
    x1_send,
    x1_recv,
    x2_send,
    x2_recv,
):
    nf, lev, rows, lanes, bands, n_lat, n_lon = dims
    groups = lev // 8
    pairs = bands // 2
    lat = lax.axis_index("lat")
    lon = lax.axis_index("lon")
    has_up = lat < n_lat - 1
    has_dn = lat > 0
    right = lax.rem(lon + 1, n_lon)
    left = lax.rem(lon + n_lon - 1, n_lon)
    up_id = {"lon": lon, "lat": lat + 1}
    dn_id = {"lon": lon, "lat": lat - 1}
    right_id = {"lon": right, "lat": lat}
    left_id = {"lon": left, "lat": lat}

    half = n_lon // 2
    place = lax.rem(lon, half)
    far_right = place == half - 1
    far_left = place == 0
    is_far = far_right | far_left
    is_near = jnp.logical_not(is_far)
    far = jnp.where(far_right, right, left)
    partner = jnp.where(far_right, left, right)
    by_right_end = place == half - 2
    by_left_end = place == 1
    is_partner = by_right_end | by_left_end
    end = jnp.where(by_right_end, right, left)
    late_half = lon >= half
    early_half = jnp.logical_not(late_half)

    def field_copy(f):
        return pltpu.make_async_copy(flat_hbm.at[f], q_buf.at[f], own_sem.at[f])

    c_copy = pltpu.make_async_copy(c_flat_hbm, c_buf, own_sem.at[nf])
    small = [
        pltpu.make_async_copy(source, target, small_sem.at[i])
        for i, (source, target) in enumerate(
            [
                (cosz_hbm, cosz_ref),
                (albedo_hbm, albedo_ref),
                (ext_hbm, ext_ref),
                (ssa_hbm, ssa_ref),
                (weight_hbm, weight_ref),
                (order_hbm, order_ref),
                (count_hbm, count_ref),
            ]
        )
    ]

    barrier = pltpu.get_barrier_semaphore()

    def greet(device):
        pl.semaphore_signal(barrier, inc=1, device_id=device, device_id_type=MESH)

    @pl.when(is_far)
    def _():
        greet({"lon": partner, "lat": lat})
        greet({"lon": far, "lat": lat})

        @pl.when(has_up)
        def _():
            greet({"lon": partner, "lat": lat + 1})

        @pl.when(has_dn)
        def _():
            greet({"lon": partner, "lat": lat - 1})

    @pl.when(is_near)
    def _():
        @pl.when(has_up)
        def _():
            greet(up_id)

        @pl.when(has_dn)
        def _():
            greet(dn_id)

        @pl.when(jnp.logical_not(by_right_end))
        def _():
            greet(right_id)

        @pl.when(jnp.logical_not(by_left_end))
        def _():
            greet(left_id)

    for f in range(nf):
        field_copy(f).start()
    c_copy.start()
    for copy in small:
        copy.start()

    n_beside = has_up.astype(jnp.int32) + has_dn.astype(jnp.int32)

    @pl.when(is_near)
    def _():
        pl.semaphore_wait(barrier, 2 + n_beside + jnp.where(is_partner, n_beside, 0))

        @pl.when(is_partner)
        def _():
            pl.semaphore_signal(
                go_sem, inc=1, device_id={"lon": end, "lat": lat}, device_id_type=MESH
            )

    @pl.when(is_far)
    def _():
        pl.semaphore_wait(go_sem, 1)

    def z1_copy(f, side, r):
        if side == 0:
            source, target, device = rows - HALO + r, r, up_id
        else:
            source, target, device = r, HALO + r, dn_id
        return pltpu.make_async_remote_copy(
            src_ref=fields_hbm.at[f, :, source, 0],
            dst_ref=q_halo.at[f, target],
            send_sem=z1_send.at[side, f, r],
            recv_sem=z1_recv.at[side, f, r],
            device_id=device,
            device_id_type=MESH,
        )

    def z2_copy(f, side):
        if side == 0:
            source, target, device = rows, 0, up_id
        else:
            source, target, device = HALO, HALO + rows, dn_id
        return pltpu.make_async_remote_copy(
            src_ref=s_buf.at[f, pl.ds(source, HALO)],
            dst_ref=s_buf.at[f, pl.ds(target, HALO)],
            send_sem=z2_send.at[side, f],
            recv_sem=z2_recv.at[side, f],
            device_id=device,
            device_id_type=MESH,
        )

    cn_copy = pltpu.make_async_remote_copy(
        src_ref=courant_hbm.at[1, :, rows - 1, 0],
        dst_ref=c_north.at[0],
        send_sem=cn_send,
        recv_sem=cn_recv,
        device_id=up_id,
        device_id_type=MESH,
    )

    def x1_copy(side):
        return pltpu.make_async_remote_copy(
            src_ref=send_1.at[side],
            dst_ref=recv_1.at[side],
            send_sem=x1_send.at[side],
            recv_sem=x1_recv.at[side],
            device_id=right_id if side == 0 else left_id,
            device_id_type=MESH,
        )

    def x2_copy(n, side):
        return pltpu.make_async_remote_copy(
            src_ref=send_2.at[side, n],
            dst_ref=recv_2.at[side, n],
            send_sem=x2_send.at[side, n],
            recv_sem=x2_recv.at[side, n],
            device_id=right_id if side == 0 else left_id,
            device_id_type=MESH,
        )

    @pl.when(has_up)
    def _():
        cn_copy.start()

    def z1_start(f):
        @pl.when(has_up)
        def _():
            for r in range(HALO):
                z1_copy(f, 0, r).start()

        @pl.when(has_dn)
        def _():
            for r in range(HALO):
                z1_copy(f, 1, r).start()

    early = jnp.where(is_near, nf, jnp.where(late_half, EARLY_SECOND, EARLY_FIRST))
    pl.loop(0, early)(z1_start)

    zero = jnp.zeros((8, lanes), jnp.float32)

    def fill_zero(ref):
        for g in range(groups):
            ref[pl.ds(8 * g, 8), :] = zero

    @pl.when(jnp.logical_not(has_dn))
    def _():
        fill_zero(c_north.at[0])

        @pl.loop(0, nf)
        def _(f):
            for r in range(HALO):
                fill_zero(q_halo.at[f, r])
                fill_zero(s_buf.at[f, r])

    @pl.when(jnp.logical_not(has_up))
    def _():
        @pl.loop(0, nf)
        def _(f):
            for r in range(HALO):
                fill_zero(q_halo.at[f, HALO + r])
                fill_zero(s_buf.at[f, HALO + rows + r])

    lane = lax.broadcasted_iota(jnp.int32, (8, lanes), 1)
    sub = lax.broadcasted_iota(jnp.int32, (8, lanes), 0)
    slot = lane >> 2
    own_half = (lane & 3) < 2
    low = sub < 4

    def pack(load):
        packed = zero
        for r in range(rows):
            for g in range(groups):
                k = r * groups + g
                packed = jnp.where(
                    slot == k, pltpu.roll(load(r, g), (4 * k + 2) % lanes, 1), packed
                )
        return packed

    def send_pair(buf, n, even, odd):
        buf[0, n] = jnp.where(own_half, even, pltpu.roll(odd, 2, 1))
        buf[1, n] = jnp.where(own_half, pltpu.roll(even, lanes - 2, 1), odd)

    def recv_pair(buf, n, odd):
        from_left = buf[0, n]
        from_right = buf[1, n]
        first = jnp.where(own_half, from_left, pltpu.roll(from_right, 2, 1))
        second = jnp.where(own_half, pltpu.roll(from_left, lanes - 2, 1), from_right)
        return jnp.where(odd, second, first)

    def own_row(f, r, g):
        return q_buf[f, pl.ds(8 * rows * g + r, 8, stride=rows), :]

    def courant_row(n, r, g):
        return c_buf[n, pl.ds(8 * rows * g + r, 8, stride=rows), :]

    @pl.loop(0, nf)
    def _(f):
        field_copy(f).wait()
        pack_q[f] = pack(lambda r, g: own_row(f, r, g))

    c_copy.wait()
    pairs_f = nf // 2
    c_pack = pack(lambda r, g: courant_row(0, r, g))
    for n in range(pairs_f):
        send_pair(send_1, n, pack_q[2 * n], pack_q[2 * n + 1])
    send_pair(send_1, pairs_f, c_pack, c_pack)
    c_edge[0] = c_pack * (1.0 / 12.0)

    for side in range(2):
        @pl.when(jnp.logical_not(far_right if side == 0 else far_left))
        def _():
            x1_copy(side).start()

    def send_far(where):
        @pl.when(where & is_far)
        def _():
            pl.semaphore_wait(barrier, 1)

        for side in range(2):
            @pl.when(where & (far_right if side == 0 else far_left))
            def _():
                x1_copy(side).start()

        @pl.when(where & is_far)
        def _():
            pl.loop(early, nf)(z1_start)

    send_far(late_half)

    ahead = lax.broadcasted_iota(jnp.int32, (2 * lanes, 2 * lanes), 0) & (lanes - 1)
    column = lax.broadcasted_iota(jnp.int32, (2 * lanes, 2 * lanes), 1)
    ahead = ahead - jnp.where(column < lanes, column, column - lanes - 1)
    inner = (ahead == 0) | (ahead == 1)
    outer = (ahead == -1) | (ahead == 2)
    band[...] = jnp.where(inner, 7.0, jnp.where(outer, -1.0, 0.0)).astype(jnp.bfloat16)

    for copy in small:
        copy.wait()
    cosz = jnp.concatenate([cosz_ref[...], cosz_ref[...]], axis=0)
    albedo = jnp.concatenate([albedo_ref[...], albedo_ref[...]], axis=0)
    neg_inv_mu = -1.0 / cosz
    ext = [
        jnp.where(low, ext_ref[2 * p], ext_ref[2 * p + 1]) * (4.0 / lev) for p in range(pairs)
    ]
    half_ssa = [jnp.where(low, ssa_ref[2 * p], ssa_ref[2 * p + 1]) * 0.5 for p in range(pairs)]
    weight = [jnp.where(low, weight_ref[2 * p], weight_ref[2 * p + 1]) for p in range(pairs)]

    ranks = lax.broadcasted_iota(jnp.int32, (lanes, lanes), 1)
    columns = lax.broadcasted_iota(jnp.int32, (lanes, lanes), 0)
    ones = jnp.ones((8, lanes), jnp.float32)
    sunlit = zero
    for r in range(rows):
        hit = (order_ref[r] == columns) & (ranks < count_ref[r])
        row = lax.dot_general(
            ones,
            hit.astype(jnp.float32),
            (((1,), (1,)), ((), ())),
            preferred_element_type=jnp.float32,
        )
        sunlit = jnp.where((sub & 3) == r, row, sunlit)
    sunlit = sunlit * float(lev)

    def optics(k, beam):
        raw = q_buf[1, pl.ds(pl.multiple_of(8 * k, 8), 8), :]
        water = jnp.maximum(raw, 0.0) + jnp.log1p(jnp.exp(-jnp.abs(raw)))
        turned = pltpu.roll(water, 4, 0)
        for half in range(2):
            level = 2 * k + half
            here = jnp.where(low, water, turned) if half == 0 else jnp.where(low, turned, water)
            after = []
            for p in range(pairs):
                tau = ext[p] * here
                direct = jnp.exp(tau * neg_inv_mu)
                decay = jnp.exp(tau * -1.66)
                rad_a[level, p] = decay
                rad_b[level, p] = half_ssa[p] * (beam[p] * (1.0 - direct))
                rad_g[level, p] = beam[p]
                after.append(beam[p] * direct)
            beam = tuple(after)
        return beam

    beam = lax.fori_loop(0, lev // 2, optics, tuple(cosz for _ in range(pairs)))

    def up_level(i, carry):
        level = lev - 1 - i
        a_below, b_below = carry
        a_out, b_out = [], []
        for p in range(pairs):
            decay = rad_a[level, p]
            source = rad_b[level, p]
            reflect = half_ssa[p] * (1.0 - decay)
            transmit = decay + reflect
            inv = 1.0 / (1.0 - reflect * a_below[p])
            through = transmit * inv
            a_here = reflect + transmit * through * a_below[p]
            b_here = through * (a_below[p] * source + b_below[p]) + source
            rad_a[level, p] = through
            rad_b[level, p] = (reflect * b_below[p] + source) * inv
            rad_c[level, p] = weight[p] * (1.0 - a_here)
            rad_g[level, p] = weight[p] * (rad_g[level, p] - b_here)
            a_out.append(a_here)
            b_out.append(b_here)
        return tuple(a_out), tuple(b_out)

    floor_b = tuple(albedo * beam[p] for p in range(pairs))
    for p in range(pairs):
        rad_c[lev, p] = weight[p] * (1.0 - albedo)
        rad_g[lev, p] = weight[p] * (beam[p] - floor_b[p])
    lax.fori_loop(0, lev, up_level, (tuple(albedo for _ in range(pairs)), floor_b))

    def net_flux(level, down):
        total = rad_c[level, 0] * down[0] + rad_g[level, 0]
        for p in range(1, pairs):
            total = total + (rad_c[level, p] * down[p] + rad_g[level, p])
        return total + pltpu.roll(total, 4, 0)

    def down_pair(k, carry):
        down, net = carry
        heats = []
        for half in range(2):
            level = 2 * k + half
            down = tuple(rad_a[level, p] * down[p] + rad_b[level, p] for p in range(pairs))
            below = net_flux(level + 1, down)
            heats.append((net - below) * sunlit)
            net = below
        heat_ref[pl.ds(pl.multiple_of(8 * k, 8), 8), :] = jnp.where(low, heats[0], heats[1])
        return down, net

    start = tuple(zero for _ in range(pairs))
    lax.fori_loop(0, lev // 2, down_pair, (start, net_flux(0, start)))
    send_far(early_half)

    @pl.when(has_dn)
    def _():
        cn_copy.wait_recv()

    for r in range(rows):
        for g in range(groups):
            here = courant_row(0, r, g) * (1.0 / 12.0)
            c_east[r, pl.ds(8 * g, 8), :] = here
            c_west[r, pl.ds(8 * g, 8), :] = jnp.where(lane == 0, 0.0, pltpu.roll(here, 1, 1))
            c_north[r + 1, pl.ds(8 * g, 8), :] = courant_row(1, r, g) * (1.0 / 12.0)
    for g in range(groups):
        c_north[0, pl.ds(8 * g, 8), :] = c_north[0, pl.ds(8 * g, 8), :] * (1.0 / 12.0)

    def tendency(load, emit):
        x = jnp.concatenate(
            [load(HALO + r, g) for r in range(rows) for g in range(groups)], axis=0
        )
        upper = x.astype(jnp.bfloat16)
        lower = (x - upper.astype(jnp.float32)).astype(jnp.bfloat16)
        flux = jnp.dot(
            jnp.concatenate([upper, lower], axis=1),
            band[...],
            preferred_element_type=jnp.float32,
        )
        for g in range(groups):
            at = pl.ds(8 * g, 8)
            q = [load(j, g) for j in range(rows + 2 * HALO)]
            north = [
                c_north[j, at, :] * (7.0 * (q[j + 1] + q[j + 2]) - (q[j] + q[j + 3]))
                for j in range(rows + 1)
            ]
            for r in range(rows):
                k = r * groups + g
                east = c_east[r, at, :] * flux[8 * k : 8 * k + 8, :lanes]
                west = c_west[r, at, :] * flux[8 * k : 8 * k + 8, lanes:]
                emit(r, g, q[r + HALO], (north[r] - north[r + 1]) - (east - west))

    corner = lane & 3

    def edge(halo, own):
        m1 = pltpu.roll(halo, 1, 1)
        m2 = pltpu.roll(halo, 2, 1)
        p1 = pltpu.roll(halo, lanes - 1, 1)
        p2 = pltpu.roll(halo, lanes - 2, 1)
        beside = pltpu.roll(own, lanes - 1, 1)
        east = jnp.where(
            corner == 0,
            -p2,
            jnp.where(corner == 1, 7.0 * p1 - p2, jnp.where(corner == 2, -m1, 0.0)),
        )
        west = jnp.where(
            corner == 0,
            0.0,
            jnp.where(
                corner == 1,
                -p1,
                jnp.where(corner == 2, 7.0 * (m1 + own) - (m2 + beside), -m2),
            ),
        )
        return c_edge[1] * west - c_edge[0] * east

    edge_lanes = (lane < 2) | (lane >= lanes - 2)

    def spread(packed, k):
        return jnp.where(edge_lanes, pltpu.roll(packed, (lanes - 2 - 4 * k) % lanes, 1), 0.0)

    def x1_wait():
        x1_copy(0).wait_recv()
        x1_copy(1).wait_recv()
        beyond = recv_pair(recv_1, pairs_f, False) * (1.0 / 12.0)
        c_edge[1] = jnp.where(
            corner == 2, pltpu.roll(beyond, 1, 1), pltpu.roll(c_edge[0], 1, 1)
        )

    def z1_wait(f):
        @pl.when(has_dn)
        def _():
            for r in range(HALO):
                z1_copy(f, 0, r).wait_recv()

        @pl.when(has_up)
        def _():
            for r in range(HALO):
                z1_copy(f, 1, r).wait_recv()

    def add_edge(f):
        change = edge(recv_pair(recv_1, f // 2, f % 2 == 1), pack_q[f])
        edge_buf[f] = change
        pack_s[f] = pack_s[f] + change

        @pl.when(f % 2 == 1)
        def _():
            n = f // 2
            send_pair(send_2, n, pack_s[f - 1], pack_s[f])
            x2_copy(n, 0).start()
            x2_copy(n, 1).start()

    def spread_edge(f):
        change = edge_buf[f]
        for r in range(rows):
            for g in range(groups):
                at = pl.ds(8 * g, 8)
                s_buf[f, HALO + r, at, :] = s_buf[f, HALO + r, at, :] + spread(
                    change, r * groups + g
                )

    def z2_start(f):
        @pl.when(has_up)
        def _():
            z2_copy(f, 0).start()

        @pl.when(has_dn)
        def _():
            z2_copy(f, 1).start()

    pl.when(is_near)(x1_wait)
    held = nf - 2

    @pl.loop(0, nf)
    def _(f):
        z1_wait(f)

        def load(j, g):
            at = pl.ds(8 * g, 8)
            if j < HALO:
                return q_halo[f, j, at, :]
            if j < HALO + rows:
                return own_row(f, j - HALO, g)
            return q_halo[f, j - rows, at, :]

        parts = [zero] * rows

        def emit(r, g, here, change):
            k = r * groups + g
            value = here + change
            s_buf[f, HALO + r, pl.ds(8 * g, 8), :] = value
            parts[r] = jnp.where(slot == k, pltpu.roll(value, (4 * k + 2) % lanes, 1), parts[r])

        tendency(load, emit)
        pack_s[f] = sum(parts[1:], parts[0])

        @pl.when(is_near)
        def _():
            add_edge(f)
            spread_edge(f)
            z2_start(f)

        @pl.when(is_far & (f == held - 1))
        def _():
            x1_wait()
            pl.loop(0, held)(add_edge)
            pl.loop(0, held)(spread_edge)

        @pl.when(is_far & (f >= held))
        def _():
            add_edge(f)

    @pl.when(is_far)
    def _():
        pl.loop(0, held)(z2_start)

        @pl.loop(held, nf)
        def _(f):
            spread_edge(f)
            z2_start(f)

    def x2_wait(n):
        x2_copy(n, 0).wait_recv()
        x2_copy(n, 1).wait_recv()

    def second_edge(f):
        return edge(recv_pair(recv_2, f // 2, f % 2 == 1), pack_s[f])

    def out_rows(r, g):
        return pl.ds(8 * rows * g + r, 8, stride=rows)

    @pl.loop(0, nf)
    def _(f):
        @pl.when(f % 2 == 0)
        def _():
            x2_wait(f // 2)

        @pl.when(has_dn)
        def _():
            z2_copy(f, 0).wait_recv()

        @pl.when(has_up)
        def _():
            z2_copy(f, 1).wait_recv()

        beyond = second_edge(f)

        def emit(r, g, here, change):
            total = (own_row(f, r, g) + here) + (change + spread(beyond, r * groups + g))
            out_ref[f, out_rows(r, g), :] = 0.5 * total

        tendency(lambda j, g: s_buf[f, j, pl.ds(8 * g, 8), :], emit)

        @pl.when(f == 0)
        def _():
            for i in range(rows * groups):
                at = pl.ds(8 * i, 8)
                out_ref[0, at, :] = out_ref[0, at, :] + 0.5 * heat_ref[at, :]

    @pl.loop(0, nf)
    def _(f):
        @pl.when(has_up)
        def _():
            for r in range(HALO):
                z1_copy(f, 0, r).wait_send()
            z2_copy(f, 0).wait_send()

        @pl.when(has_dn)
        def _():
            for r in range(HALO):
                z1_copy(f, 1, r).wait_send()
            z2_copy(f, 1).wait_send()

    @pl.when(has_up)
    def _():
        cn_copy.wait_send()

    for side in range(2):
        x1_copy(side).wait_send()
        for n in range(pairs_f):
            x2_copy(n, side).wait_send()


def store_kernel(parts, new_ref, heat_ref, new_hbm, out_heat_hbm, sem):
    copies = [
        pltpu.make_async_copy(new_ref.at[f], new_hbm.at[f], sem.at[f]) for f in range(parts)
    ]
    copies.append(pltpu.make_async_copy(heat_ref, out_heat_hbm, sem.at[parts]))
    for copy in copies:
        copy.start()
    for copy in copies:
        copy.wait()


def per_device(n_lat, n_lon, fields, courant, cosz, albedo, ext, ssa, weight, order, count):
    nf, lev, rows, lanes = fields.shape
    bands = ext.shape[0]
    dims = (nf, lev, rows, lanes, bands, n_lat, n_lon)
    tall = rows + 2 * HALO
    f32 = jnp.float32
    hbm_spec = pl.BlockSpec(memory_space=pltpu.HBM)
    vmem_spec = pl.BlockSpec(memory_space=pltpu.VMEM)
    rad = pltpu.VMEM((lev + 1, bands // 2, 8, lanes), f32)
    pairs_f = nf // 2
    results = (
        jax.ShapeDtypeStruct((nf, lev * rows, lanes), f32),
        jax.ShapeDtypeStruct((lev * rows, lanes), f32),
    )
    out, heat = pl.pallas_call(
        functools.partial(step_kernel, dims),
        out_shape=(
            pltpu.VMEM((nf, lev * rows, lanes), f32),
            pltpu.VMEM((lev * rows, lanes), f32),
        ),
        in_specs=[hbm_spec] * 11,
        out_specs=(vmem_spec, vmem_spec),
        scratch_shapes=[
            pltpu.VMEM((nf, lev * rows, lanes), f32),
            pltpu.VMEM((nf, 2 * HALO, lev, lanes), f32),
            pltpu.VMEM((nf, tall, lev, lanes), f32),
            pltpu.VMEM((2, lev * rows, lanes), f32),
            pltpu.VMEM((rows, lev, lanes), f32),
            pltpu.VMEM((rows, lev, lanes), f32),
            pltpu.VMEM((rows + 1, lev, lanes), f32),
            pltpu.VMEM((rows, lanes), f32),
            pltpu.VMEM((rows, lanes), f32),
            pltpu.SMEM((bands,), f32),
            pltpu.SMEM((bands,), f32),
            pltpu.SMEM((bands,), f32),
            pltpu.VMEM((rows, 1, lanes), jnp.int32),
            pltpu.SMEM((rows,), jnp.int32),
            rad,
            rad,
            rad,
            rad,
            pltpu.VMEM((2 * lanes, 2 * lanes), jnp.bfloat16),
            pltpu.VMEM((2, 8, lanes), f32),
            pltpu.VMEM((nf, 8, lanes), f32),
            pltpu.VMEM((nf, 8, lanes), f32),
            pltpu.VMEM((nf, 8, lanes), f32),
            pltpu.VMEM((2, pairs_f + 1, 8, lanes), f32),
            pltpu.VMEM((2, pairs_f + 1, 8, lanes), f32),
            pltpu.VMEM((2, pairs_f, 8, lanes), f32),
            pltpu.VMEM((2, pairs_f, 8, lanes), f32),
            pltpu.SemaphoreType.DMA((nf + 1,)),
            pltpu.SemaphoreType.DMA((7,)),
            pltpu.SemaphoreType.REGULAR,
            pltpu.SemaphoreType.DMA((2, nf, HALO)),
            pltpu.SemaphoreType.DMA((2, nf, HALO)),
            pltpu.SemaphoreType.DMA((2, nf)),
            pltpu.SemaphoreType.DMA((2, nf)),
            pltpu.SemaphoreType.DMA,
            pltpu.SemaphoreType.DMA,
            pltpu.SemaphoreType.DMA((2,)),
            pltpu.SemaphoreType.DMA((2,)),
            pltpu.SemaphoreType.DMA((2, pairs_f)),
            pltpu.SemaphoreType.DMA((2, pairs_f)),
        ],
        compiler_params=pltpu.CompilerParams(
            collective_id=0, has_side_effects=True, vmem_limit_bytes=48 * 1024 * 1024
        ),
        name="advect_radiate",
    )(
        *(
            pltpu.with_memory_space_constraint(x, pltpu.HBM)
            for x in (
                fields.reshape(nf, lev, rows, 1, lanes),
                fields.reshape(nf, lev * rows, lanes),
                courant.reshape(2, lev, rows, 1, lanes),
                courant.reshape(2, lev * rows, lanes),
                cosz,
                albedo,
                ext,
                ssa,
                weight,
                order,
                count.reshape(rows),
            )
        )
    )
    out, heat = pl.pallas_call(
        functools.partial(store_kernel, nf),
        out_shape=results,
        in_specs=[pl.BlockSpec(memory_space=pl.ANY)] * 2,
        out_specs=(hbm_spec, hbm_spec),
        scratch_shapes=[pltpu.SemaphoreType.DMA((nf + 1,))],
        compiler_params=pltpu.CompilerParams(vmem_limit_bytes=32 * 1024 * 1024),
        name="store_results",
    )(out, heat)
    return out.reshape(nf, lev, rows, lanes), heat.reshape(lev, rows, lanes)


def solution(mesh):
    n_lat, n_lon = mesh.shape["lat"], mesh.shape["lon"]
    in_specs = (
        P(None, None, "lat", "lon"),
        P(None, None, "lat", "lon"),
        P("lat", "lon"),
        P("lat", "lon"),
        P(),
        P(),
        P(),
        P("lat", "lon", None),
        P("lat", "lon"),
    )
    out_specs = (P(None, None, "lat", "lon"), P(None, "lat", "lon"))
    return jax.shard_map(
        functools.partial(per_device, n_lat, n_lon),
        mesh=mesh,
        in_specs=in_specs,
        out_specs=out_specs,
        check_vma=False,
    )
```

```python
import functools

import jax
import jax.numpy as jnp
from jax import lax
from jax.experimental import pallas as pl
from jax.experimental.pallas import tpu as pltpu
from jax.sharding import PartitionSpec as P

MESH = pl.DeviceIdType.MESH
HALO = 2
EARLY_FIRST = 4
EARLY_SECOND = 2


def step_kernel(
    dims,
    fields_hbm,
    flat_hbm,
    courant_hbm,
    c_flat_hbm,
    cosz_hbm,
    albedo_hbm,
    ext_hbm,
    ssa_hbm,
    weight_hbm,
    order_hbm,
    count_hbm,
    out_ref,
    heat_ref,
    q_buf,
    q_halo,
    s_buf,
    c_buf,
    c_east,
    c_west,
    c_north,
    cosz_ref,
    albedo_ref,
    ext_ref,
    ssa_ref,
    weight_ref,
    order_ref,
    count_ref,
    rad_a,
    rad_b,
    rad_c,
    rad_g,
    band,
    c_edge,
    pack_q,
    pack_s,
    edge_buf,
    send_1,
    recv_1,
    send_2,
    recv_2,
    own_sem,
    small_sem,
    go_sem,
    z1_send,
    z1_recv,
    z2_send,
    z2_recv,
    cn_send,
    cn_recv,
    x1_send,
    x1_recv,
    x2_send,
    x2_recv,
):
    nf, lev, rows, lanes, bands, n_lat, n_lon = dims
    groups = lev // 8
    pairs = bands // 2
    lat = lax.axis_index("lat")
    lon = lax.axis_index("lon")
    has_up = lat < n_lat - 1
    has_dn = lat > 0
    right = lax.rem(lon + 1, n_lon)
    left = lax.rem(lon + n_lon - 1, n_lon)
    up_id = {"lon": lon, "lat": lat + 1}
    dn_id = {"lon": lon, "lat": lat - 1}
    right_id = {"lon": right, "lat": lat}
    left_id = {"lon": left, "lat": lat}

    half = n_lon // 2
    place = lax.rem(lon, half)
    far_right = place == half - 1
    far_left = place == 0
    is_far = far_right | far_left
    is_near = jnp.logical_not(is_far)
    far = jnp.where(far_right, right, left)
    partner = jnp.where(far_right, left, right)
    by_right_end = place == half - 2
    by_left_end = place == 1
    is_partner = by_right_end | by_left_end
    end = jnp.where(by_right_end, right, left)
    late_half = lon >= half
    early_half = jnp.logical_not(late_half)

    def field_copy(f):
        return pltpu.make_async_copy(flat_hbm.at[f], q_buf.at[f], own_sem.at[f])

    c_copy = pltpu.make_async_copy(c_flat_hbm, c_buf, own_sem.at[nf])
    small = [
        pltpu.make_async_copy(source, target, small_sem.at[i])
        for i, (source, target) in enumerate(
            [
                (cosz_hbm, cosz_ref),
                (albedo_hbm, albedo_ref),
                (ext_hbm, ext_ref),
                (ssa_hbm, ssa_ref),
                (weight_hbm, weight_ref),
                (order_hbm, order_ref),
                (count_hbm, count_ref),
            ]
        )
    ]

    barrier = pltpu.get_barrier_semaphore()

    def greet(device):
        pl.semaphore_signal(barrier, inc=1, device_id=device, device_id_type=MESH)

    @pl.when(is_far)
    def _():
        greet({"lon": partner, "lat": lat})
        greet({"lon": far, "lat": lat})

        @pl.when(has_up)
        def _():
            greet({"lon": partner, "lat": lat + 1})

        @pl.when(has_dn)
        def _():
            greet({"lon": partner, "lat": lat - 1})

    @pl.when(is_near)
    def _():
        @pl.when(has_up)
        def _():
            greet(up_id)

        @pl.when(has_dn)
        def _():
            greet(dn_id)

        @pl.when(jnp.logical_not(by_right_end))
        def _():
            greet(right_id)

        @pl.when(jnp.logical_not(by_left_end))
        def _():
            greet(left_id)

    for f in range(nf):
        field_copy(f).start()
    c_copy.start()
    for copy in small:
        copy.start()

    n_beside = has_up.astype(jnp.int32) + has_dn.astype(jnp.int32)

    @pl.when(is_near)
    def _():
        pl.semaphore_wait(barrier, 2 + n_beside + jnp.where(is_partner, n_beside, 0))

        @pl.when(is_partner)
        def _():
            pl.semaphore_signal(
                go_sem, inc=1, device_id={"lon": end, "lat": lat}, device_id_type=MESH
            )

    @pl.when(is_far)
    def _():
        pl.semaphore_wait(go_sem, 1)

    def z1_copy(f, side, r):
        if side == 0:
            source, target, device = rows - HALO + r, r, up_id
        else:
            source, target, device = r, HALO + r, dn_id
        return pltpu.make_async_remote_copy(
            src_ref=fields_hbm.at[f, :, source, 0],
            dst_ref=q_halo.at[f, target],
            send_sem=z1_send.at[side, f, r],
            recv_sem=z1_recv.at[side, f, r],
            device_id=device,
            device_id_type=MESH,
        )

    def z2_copy(f, side):
        if side == 0:
            source, target, device = rows, 0, up_id
        else:
            source, target, device = HALO, HALO + rows, dn_id
        return pltpu.make_async_remote_copy(
            src_ref=s_buf.at[f, pl.ds(source, HALO)],
            dst_ref=s_buf.at[f, pl.ds(target, HALO)],
            send_sem=z2_send.at[side, f],
            recv_sem=z2_recv.at[side, f],
            device_id=device,
            device_id_type=MESH,
        )

    cn_copy = pltpu.make_async_remote_copy(
        src_ref=courant_hbm.at[1, :, rows - 1, 0],
        dst_ref=c_north.at[0],
        send_sem=cn_send,
        recv_sem=cn_recv,
        device_id=up_id,
        device_id_type=MESH,
    )

    def x1_copy(side):
        return pltpu.make_async_remote_copy(
            src_ref=send_1.at[side],
            dst_ref=recv_1.at[side],
            send_sem=x1_send.at[side],
            recv_sem=x1_recv.at[side],
            device_id=right_id if side == 0 else left_id,
            device_id_type=MESH,
        )

    def x2_copy(n, side):
        return pltpu.make_async_remote_copy(
            src_ref=send_2.at[side, n],
            dst_ref=recv_2.at[side, n],
            send_sem=x2_send.at[side, n],
            recv_sem=x2_recv.at[side, n],
            device_id=right_id if side == 0 else left_id,
            device_id_type=MESH,
        )

    @pl.when(has_up)
    def _():
        cn_copy.start()

    def z1_start(f):
        @pl.when(has_up)
        def _():
            for r in range(HALO):
                z1_copy(f, 0, r).start()

        @pl.when(has_dn)
        def _():
            for r in range(HALO):
                z1_copy(f, 1, r).start()

    early = jnp.where(is_near, nf, jnp.where(late_half, EARLY_SECOND, EARLY_FIRST))
    pl.loop(0, early)(z1_start)

    zero = jnp.zeros((8, lanes), jnp.float32)

    def fill_zero(ref):
        for g in range(groups):
            ref[pl.ds(8 * g, 8), :] = zero

    @pl.when(jnp.logical_not(has_dn))
    def _():
        fill_zero(c_north.at[0])

        @pl.loop(0, nf)
        def _(f):
            for r in range(HALO):
                fill_zero(q_halo.at[f, r])
                fill_zero(s_buf.at[f, r])

    @pl.when(jnp.logical_not(has_up))
    def _():
        @pl.loop(0, nf)
        def _(f):
            for r in range(HALO):
                fill_zero(q_halo.at[f, HALO + r])
                fill_zero(s_buf.at[f, HALO + rows + r])

    lane = lax.broadcasted_iota(jnp.int32, (8, lanes), 1)
    sub = lax.broadcasted_iota(jnp.int32, (8, lanes), 0)
    slot = lane >> 2
    own_half = (lane & 3) < 2
    low = sub < 4

    def pack(load):
        packed = zero
        for r in range(rows):
            for g in range(groups):
                k = r * groups + g
                packed = jnp.where(
                    slot == k, pltpu.roll(load(r, g), (4 * k + 2) % lanes, 1), packed
                )
        return packed

    def send_pair(buf, n, even, odd):
        buf[0, n] = jnp.where(own_half, even, pltpu.roll(odd, 2, 1))
        buf[1, n] = jnp.where(own_half, pltpu.roll(even, lanes - 2, 1), odd)

    def recv_pair(buf, n, odd):
        from_left = buf[0, n]
        from_right = buf[1, n]
        first = jnp.where(own_half, from_left, pltpu.roll(from_right, 2, 1))
        second = jnp.where(own_half, pltpu.roll(from_left, lanes - 2, 1), from_right)
        return jnp.where(odd, second, first)

    def own_row(f, r, g):
        return q_buf[f, pl.ds(8 * rows * g + r, 8, stride=rows), :]

    def courant_row(n, r, g):
        return c_buf[n, pl.ds(8 * rows * g + r, 8, stride=rows), :]

    @pl.loop(0, nf)
    def _(f):
        field_copy(f).wait()
        pack_q[f] = pack(lambda r, g: own_row(f, r, g))

    c_copy.wait()
    pairs_f = nf // 2
    c_pack = pack(lambda r, g: courant_row(0, r, g))
    for n in range(pairs_f):
        send_pair(send_1, n, pack_q[2 * n], pack_q[2 * n + 1])
    send_pair(send_1, pairs_f, c_pack, c_pack)
    c_edge[0] = c_pack * (1.0 / 12.0)

    for side in range(2):
        @pl.when(jnp.logical_not(far_right if side == 0 else far_left))
        def _():
            x1_copy(side).start()

    def send_far(where):
        @pl.when(where & is_far)
        def _():
            pl.semaphore_wait(barrier, 1)

        for side in range(2):
            @pl.when(where & (far_right if side == 0 else far_left))
            def _():
                x1_copy(side).start()

        @pl.when(where & is_far)
        def _():
            pl.loop(early, nf)(z1_start)

    send_far(late_half)

    ahead = lax.broadcasted_iota(jnp.int32, (2 * lanes, 2 * lanes), 0) & (lanes - 1)
    column = lax.broadcasted_iota(jnp.int32, (2 * lanes, 2 * lanes), 1)
    ahead = ahead - jnp.where(column < lanes, column, column - lanes - 1)
    inner = (ahead == 0) | (ahead == 1)
    outer = (ahead == -1) | (ahead == 2)
    band[...] = jnp.where(inner, 7.0, jnp.where(outer, -1.0, 0.0)).astype(jnp.bfloat16)

    for copy in small:
        copy.wait()
    cosz = jnp.concatenate([cosz_ref[...], cosz_ref[...]], axis=0)
    albedo = jnp.concatenate([albedo_ref[...], albedo_ref[...]], axis=0)
    neg_inv_mu = -1.0 / cosz
    ext = [
        jnp.where(low, ext_ref[2 * p], ext_ref[2 * p + 1]) * (4.0 / lev) for p in range(pairs)
    ]
    half_ssa = [jnp.where(low, ssa_ref[2 * p], ssa_ref[2 * p + 1]) * 0.5 for p in range(pairs)]
    weight = [jnp.where(low, weight_ref[2 * p], weight_ref[2 * p + 1]) for p in range(pairs)]

    ranks = lax.broadcasted_iota(jnp.int32, (lanes, lanes), 1)
    columns = lax.broadcasted_iota(jnp.int32, (lanes, lanes), 0)
    ones = jnp.ones((8, lanes), jnp.float32)
    sunlit = zero
    for r in range(rows):
        hit = (order_ref[r] == columns) & (ranks < count_ref[r])
        row = lax.dot_general(
            ones,
            hit.astype(jnp.float32),
            (((1,), (1,)), ((), ())),
            preferred_element_type=jnp.float32,
        )
        sunlit = jnp.where((sub & 3) == r, row, sunlit)
    sunlit = sunlit * float(lev)

    def optics(k, beam):
        raw = q_buf[1, pl.ds(pl.multiple_of(8 * k, 8), 8), :]
        water = jnp.maximum(raw, 0.0) + jnp.log1p(jnp.exp(-jnp.abs(raw)))
        turned = pltpu.roll(water, 4, 0)
        for half in range(2):
            level = 2 * k + half
            here = jnp.where(low, water, turned) if half == 0 else jnp.where(low, turned, water)
            after = []
            for p in range(pairs):
                tau = ext[p] * here
                direct = jnp.exp(tau * neg_inv_mu)
                decay = jnp.exp(tau * -1.66)
                rad_a[level, p] = decay
                rad_b[level, p] = half_ssa[p] * (beam[p] * (1.0 - direct))
                rad_g[level, p] = beam[p]
                after.append(beam[p] * direct)
            beam = tuple(after)
        return beam

    beam = lax.fori_loop(0, lev // 2, optics, tuple(cosz for _ in range(pairs)))

    def up_level(i, carry):
        level = lev - 1 - i
        a_below, b_below = carry
        a_out, b_out = [], []
        for p in range(pairs):
            decay = rad_a[level, p]
            source = rad_b[level, p]
            reflect = half_ssa[p] * (1.0 - decay)
            transmit = decay + reflect
            inv = 1.0 / (1.0 - reflect * a_below[p])
            through = transmit * inv
            a_here = reflect + transmit * through * a_below[p]
            b_here = through * (a_below[p] * source + b_below[p]) + source
            rad_a[level, p] = through
            rad_b[level, p] = (reflect * b_below[p] + source) * inv
            rad_c[level, p] = weight[p] * (1.0 - a_here)
            rad_g[level, p] = weight[p] * (rad_g[level, p] - b_here)
            a_out.append(a_here)
            b_out.append(b_here)
        return tuple(a_out), tuple(b_out)

    floor_b = tuple(albedo * beam[p] for p in range(pairs))
    for p in range(pairs):
        rad_c[lev, p] = weight[p] * (1.0 - albedo)
        rad_g[lev, p] = weight[p] * (beam[p] - floor_b[p])
    lax.fori_loop(0, lev, up_level, (tuple(albedo for _ in range(pairs)), floor_b))

    def net_flux(level, down):
        total = rad_c[level, 0] * down[0] + rad_g[level, 0]
        for p in range(1, pairs):
            total = total + (rad_c[level, p] * down[p] + rad_g[level, p])
        return total + pltpu.roll(total, 4, 0)

    def down_pair(k, carry):
        down, net = carry
        heats = []
        for half in range(2):
            level = 2 * k + half
            down = tuple(rad_a[level, p] * down[p] + rad_b[level, p] for p in range(pairs))
            below = net_flux(level + 1, down)
            heats.append((net - below) * sunlit)
            net = below
        heat_ref[pl.ds(pl.multiple_of(8 * k, 8), 8), :] = jnp.where(low, heats[0], heats[1])
        return down, net

    start = tuple(zero for _ in range(pairs))
    lax.fori_loop(0, lev // 2, down_pair, (start, net_flux(0, start)))
    send_far(early_half)

    @pl.when(has_dn)
    def _():
        cn_copy.wait_recv()

    for r in range(rows):
        for g in range(groups):
            here = courant_row(0, r, g) * (1.0 / 12.0)
            c_east[r, pl.ds(8 * g, 8), :] = here
            c_west[r, pl.ds(8 * g, 8), :] = jnp.where(lane == 0, 0.0, pltpu.roll(here, 1, 1))
            c_north[r + 1, pl.ds(8 * g, 8), :] = courant_row(1, r, g) * (1.0 / 12.0)
    for g in range(groups):
        c_north[0, pl.ds(8 * g, 8), :] = c_north[0, pl.ds(8 * g, 8), :] * (1.0 / 12.0)

    def tendency(load, emit):
        x = jnp.concatenate(
            [load(HALO + r, g) for r in range(rows) for g in range(groups)], axis=0
        )
        upper = x.astype(jnp.bfloat16)
        lower = (x - upper.astype(jnp.float32)).astype(jnp.bfloat16)
        flux = jnp.dot(
            jnp.concatenate([upper, lower], axis=1),
            band[...],
            preferred_element_type=jnp.float32,
        )
        for g in range(groups):
            at = pl.ds(8 * g, 8)
            q = [load(j, g) for j in range(rows + 2 * HALO)]
            north = [
                c_north[j, at, :] * (7.0 * (q[j + 1] + q[j + 2]) - (q[j] + q[j + 3]))
                for j in range(rows + 1)
            ]
            for r in range(rows):
                k = r * groups + g
                east = c_east[r, at, :] * flux[8 * k : 8 * k + 8, :lanes]
                west = c_west[r, at, :] * flux[8 * k : 8 * k + 8, lanes:]
                emit(r, g, q[r + HALO], (north[r] - north[r + 1]) - (east - west))

    corner = lane & 3

    def edge(halo, own):
        m1 = pltpu.roll(halo, 1, 1)
        m2 = pltpu.roll(halo, 2, 1)
        p1 = pltpu.roll(halo, lanes - 1, 1)
        p2 = pltpu.roll(halo, lanes - 2, 1)
        beside = pltpu.roll(own, lanes - 1, 1)
        east = jnp.where(
            corner == 0,
            -p2,
            jnp.where(corner == 1, 7.0 * p1 - p2, jnp.where(corner == 2, -m1, 0.0)),
        )
        west = jnp.where(
            corner == 0,
            0.0,
            jnp.where(
                corner == 1,
                -p1,
                jnp.where(corner == 2, 7.0 * (m1 + own) - (m2 + beside), -m2),
            ),
        )
        return c_edge[1] * west - c_edge[0] * east

    edge_lanes = (lane < 2) | (lane >= lanes - 2)

    def spread(packed, k):
        return jnp.where(edge_lanes, pltpu.roll(packed, (lanes - 2 - 4 * k) % lanes, 1), 0.0)

    def x1_wait():
        x1_copy(0).wait_recv()
        x1_copy(1).wait_recv()
        beyond = recv_pair(recv_1, pairs_f, False) * (1.0 / 12.0)
        c_edge[1] = jnp.where(
            corner == 2, pltpu.roll(beyond, 1, 1), pltpu.roll(c_edge[0], 1, 1)
        )

    def z1_wait(f):
        @pl.when(has_dn)
        def _():
            for r in range(HALO):
                z1_copy(f, 0, r).wait_recv()

        @pl.when(has_up)
        def _():
            for r in range(HALO):
                z1_copy(f, 1, r).wait_recv()

    def add_edge(f):
        change = edge(recv_pair(recv_1, f // 2, f % 2 == 1), pack_q[f])
        edge_buf[f] = change
        pack_s[f] = pack_s[f] + change

        @pl.when(f % 2 == 1)
        def _():
            n = f // 2
            send_pair(send_2, n, pack_s[f - 1], pack_s[f])
            x2_copy(n, 0).start()
            x2_copy(n, 1).start()

    def spread_edge(f):
        change = edge_buf[f]
        for r in range(rows):
            for g in range(groups):
                at = pl.ds(8 * g, 8)
                s_buf[f, HALO + r, at, :] = s_buf[f, HALO + r, at, :] + spread(
                    change, r * groups + g
                )

    def z2_start(f):
        @pl.when(has_up)
        def _():
            z2_copy(f, 0).start()

        @pl.when(has_dn)
        def _():
            z2_copy(f, 1).start()

    pl.when(is_near)(x1_wait)
    held = nf - 2

    @pl.loop(0, nf)
    def _(f):
        z1_wait(f)

        def load(j, g):
            at = pl.ds(8 * g, 8)
            if j < HALO:
                return q_halo[f, j, at, :]
            if j < HALO + rows:
                return own_row(f, j - HALO, g)
            return q_halo[f, j - rows, at, :]

        parts = [zero] * rows

        def emit(r, g, here, change):
            k = r * groups + g
            value = here + change
            s_buf[f, HALO + r, pl.ds(8 * g, 8), :] = value
            parts[r] = jnp.where(slot == k, pltpu.roll(value, (4 * k + 2) % lanes, 1), parts[r])

        tendency(load, emit)
        pack_s[f] = sum(parts[1:], parts[0])

        @pl.when(is_near)
        def _():
            add_edge(f)
            spread_edge(f)
            z2_start(f)

        @pl.when(is_far & (f == held - 1))
        def _():
            x1_wait()
            pl.loop(0, held)(add_edge)
            pl.loop(0, held)(spread_edge)

        @pl.when(is_far & (f >= held))
        def _():
            add_edge(f)

    @pl.when(is_far)
    def _():
        pl.loop(0, held)(z2_start)

        @pl.loop(held, nf)
        def _(f):
            spread_edge(f)
            z2_start(f)

    def x2_wait(n):
        x2_copy(n, 0).wait_recv()
        x2_copy(n, 1).wait_recv()

    def z2_sent(f):
        @pl.when(has_up)
        def _():
            z2_copy(f, 0).wait_send()

        @pl.when(has_dn)
        def _():
            z2_copy(f, 1).wait_send()

    def second_edge(f):
        return edge(recv_pair(recv_2, f // 2, f % 2 == 1), pack_s[f])

    def out_rows(r, g):
        return pl.ds(8 * rows * g + r, 8, stride=rows)

    def z2_wait(f):
        @pl.when(has_dn)
        def _():
            z2_copy(f, 0).wait_recv()

        @pl.when(has_up)
        def _():
            z2_copy(f, 1).wait_recv()

    def final(f, load):
        beyond = second_edge(f)

        def emit(r, g, here, change):
            total = (own_row(f, r, g) + here) + (change + spread(beyond, r * groups + g))
            out_ref[f, out_rows(r, g), :] = 0.5 * total

        tendency(load, emit)

    @pl.loop(0, nf)
    def _(f):
        @pl.when(has_up)
        def _():
            for r in range(HALO):
                z1_copy(f, 0, r).wait_send()

        @pl.when(has_dn)
        def _():
            for r in range(HALO):
                z1_copy(f, 1, r).wait_send()

    @pl.when(has_up)
    def _():
        cn_copy.wait_send()

    for side in range(2):
        x1_copy(side).wait_send()

    @pl.loop(0, nf - 1)
    def _(f):
        @pl.when(f % 2 == 0)
        def _():
            x2_wait(f // 2)
            x2_copy(f // 2, 0).wait_send()
            x2_copy(f // 2, 1).wait_send()

        @pl.when(f > 0)
        def _():
            z2_sent(f - 1)

        z2_wait(f)
        final(f, lambda j, g: s_buf[f, j, pl.ds(8 * g, 8), :])

        @pl.when(f == 0)
        def _():
            for i in range(rows * groups):
                at = pl.ds(8 * i, 8)
                out_ref[0, at, :] = out_ref[0, at, :] + 0.5 * heat_ref[at, :]

    last = nf - 1

    def inner_row(j, g):
        if j < HALO or j >= HALO + rows:
            return zero
        return s_buf[last, j, pl.ds(8 * g, 8), :]

    z2_sent(last - 1)
    final(last, inner_row)
    z2_wait(last)
    top = HALO + rows
    for g in range(groups):
        at = pl.ds(8 * g, 8)
        below = s_buf[last, HALO - 1, at, :]
        above = s_buf[last, top, at, :]
        low_face = c_north[0, at, :] * (7.0 * below - s_buf[last, HALO - 2, at, :])
        high_face = c_north[rows, at, :] * (7.0 * above - s_buf[last, top + 1, at, :])
        low_next = c_north[1, at, :] * below
        high_next = c_north[rows - 1, at, :] * above
        terms = {0: low_face + low_next, 1: -low_next}
        for r, term in ((rows - 2, high_next), (rows - 1, -high_next - high_face)):
            terms[r] = terms[r] + term if r in terms else term
        for r in sorted(terms):
            rows_at = out_rows(r, g)
            out_ref[last, rows_at, :] = out_ref[last, rows_at, :] + 0.5 * terms[r]

    z2_sent(last)


def store_kernel(parts, new_ref, heat_ref, new_hbm, out_heat_hbm, sem):
    copies = [
        pltpu.make_async_copy(new_ref.at[f], new_hbm.at[f], sem.at[f]) for f in range(parts)
    ]
    copies.append(pltpu.make_async_copy(heat_ref, out_heat_hbm, sem.at[parts]))
    for copy in copies:
        copy.start()
    for copy in copies:
        copy.wait()


def per_device(n_lat, n_lon, fields, courant, cosz, albedo, ext, ssa, weight, order, count):
    nf, lev, rows, lanes = fields.shape
    bands = ext.shape[0]
    dims = (nf, lev, rows, lanes, bands, n_lat, n_lon)
    tall = rows + 2 * HALO
    f32 = jnp.float32
    hbm_spec = pl.BlockSpec(memory_space=pltpu.HBM)
    vmem_spec = pl.BlockSpec(memory_space=pltpu.VMEM)
    rad = pltpu.VMEM((lev + 1, bands // 2, 8, lanes), f32)
    pairs_f = nf // 2
    results = (
        jax.ShapeDtypeStruct((nf, lev * rows, lanes), f32),
        jax.ShapeDtypeStruct((lev * rows, lanes), f32),
    )
    out, heat = pl.pallas_call(
        functools.partial(step_kernel, dims),
        out_shape=(
            pltpu.VMEM((nf, lev * rows, lanes), f32),
            pltpu.VMEM((lev * rows, lanes), f32),
        ),
        in_specs=[hbm_spec] * 11,
        out_specs=(vmem_spec, vmem_spec),
        scratch_shapes=[
            pltpu.VMEM((nf, lev * rows, lanes), f32),
            pltpu.VMEM((nf, 2 * HALO, lev, lanes), f32),
            pltpu.VMEM((nf, tall, lev, lanes), f32),
            pltpu.VMEM((2, lev * rows, lanes), f32),
            pltpu.VMEM((rows, lev, lanes), f32),
            pltpu.VMEM((rows, lev, lanes), f32),
            pltpu.VMEM((rows + 1, lev, lanes), f32),
            pltpu.VMEM((rows, lanes), f32),
            pltpu.VMEM((rows, lanes), f32),
            pltpu.SMEM((bands,), f32),
            pltpu.SMEM((bands,), f32),
            pltpu.SMEM((bands,), f32),
            pltpu.VMEM((rows, 1, lanes), jnp.int32),
            pltpu.SMEM((rows,), jnp.int32),
            rad,
            rad,
            rad,
            rad,
            pltpu.VMEM((2 * lanes, 2 * lanes), jnp.bfloat16),
            pltpu.VMEM((2, 8, lanes), f32),
            pltpu.VMEM((nf, 8, lanes), f32),
            pltpu.VMEM((nf, 8, lanes), f32),
            pltpu.VMEM((nf, 8, lanes), f32),
            pltpu.VMEM((2, pairs_f + 1, 8, lanes), f32),
            pltpu.VMEM((2, pairs_f + 1, 8, lanes), f32),
            pltpu.VMEM((2, pairs_f, 8, lanes), f32),
            pltpu.VMEM((2, pairs_f, 8, lanes), f32),
            pltpu.SemaphoreType.DMA((nf + 1,)),
            pltpu.SemaphoreType.DMA((7,)),
            pltpu.SemaphoreType.REGULAR,
            pltpu.SemaphoreType.DMA((2, nf, HALO)),
            pltpu.SemaphoreType.DMA((2, nf, HALO)),
            pltpu.SemaphoreType.DMA((2, nf)),
            pltpu.SemaphoreType.DMA((2, nf)),
            pltpu.SemaphoreType.DMA,
            pltpu.SemaphoreType.DMA,
            pltpu.SemaphoreType.DMA((2,)),
            pltpu.SemaphoreType.DMA((2,)),
            pltpu.SemaphoreType.DMA((2, pairs_f)),
            pltpu.SemaphoreType.DMA((2, pairs_f)),
        ],
        compiler_params=pltpu.CompilerParams(
            collective_id=0, has_side_effects=True, vmem_limit_bytes=48 * 1024 * 1024
        ),
        name="advect_radiate",
    )(
        *(
            pltpu.with_memory_space_constraint(x, pltpu.HBM)
            for x in (
                fields.reshape(nf, lev, rows, 1, lanes),
                fields.reshape(nf, lev * rows, lanes),
                courant.reshape(2, lev, rows, 1, lanes),
                courant.reshape(2, lev * rows, lanes),
                cosz,
                albedo,
                ext,
                ssa,
                weight,
                order,
                count.reshape(rows),
            )
        )
    )
    out, heat = pl.pallas_call(
        functools.partial(store_kernel, nf),
        out_shape=results,
        in_specs=[pl.BlockSpec(memory_space=pl.ANY)] * 2,
        out_specs=(hbm_spec, hbm_spec),
        scratch_shapes=[pltpu.SemaphoreType.DMA((nf + 1,))],
        compiler_params=pltpu.CompilerParams(vmem_limit_bytes=32 * 1024 * 1024),
        name="store_results",
    )(out, heat)
    return out.reshape(nf, lev, rows, lanes), heat.reshape(lev, rows, lanes)


def solution(mesh):
    n_lat, n_lon = mesh.shape["lat"], mesh.shape["lon"]
    in_specs = (
        P(None, None, "lat", "lon"),
        P(None, None, "lat", "lon"),
        P("lat", "lon"),
        P("lat", "lon"),
        P(),
        P(),
        P(),
        P("lat", "lon", None),
        P("lat", "lon"),
    )
    out_specs = (P(None, None, "lat", "lon"), P(None, "lat", "lon"))
    return jax.shard_map(
        functools.partial(per_device, n_lat, n_lon),
        mesh=mesh,
        in_specs=in_specs,
        out_specs=out_specs,
        check_vma=False,
    )
```

```python
import functools

import jax
import jax.numpy as jnp
from jax import lax
from jax.experimental import pallas as pl
from jax.experimental.pallas import tpu as pltpu
from jax.sharding import PartitionSpec as P

MESH = pl.DeviceIdType.MESH
HALO = 2
EARLY_FIRST = 4
EARLY_SECOND = 2
YIELD = 3


def step_kernel(
    dims,
    fields_hbm,
    flat_hbm,
    courant_hbm,
    c_flat_hbm,
    cosz_hbm,
    albedo_hbm,
    ext_hbm,
    ssa_hbm,
    weight_hbm,
    order_hbm,
    count_hbm,
    out_ref,
    heat_ref,
    q_buf,
    q_halo,
    s_buf,
    c_buf,
    c_east,
    c_west,
    c_north,
    cosz_ref,
    albedo_ref,
    ext_ref,
    ssa_ref,
    weight_ref,
    order_ref,
    count_ref,
    rad_a,
    rad_b,
    rad_c,
    rad_g,
    band,
    c_edge,
    pack_q,
    pack_s,
    edge_buf,
    send_1,
    recv_1,
    send_2,
    recv_2,
    own_sem,
    small_sem,
    go_sem,
    z1_send,
    z1_recv,
    z2_send,
    z2_recv,
    cn_send,
    cn_recv,
    x1_send,
    x1_recv,
    x2_send,
    x2_recv,
):
    nf, lev, rows, lanes, bands, n_lat, n_lon = dims
    groups = lev // 8
    pairs = bands // 2
    lat = lax.axis_index("lat")
    lon = lax.axis_index("lon")
    has_up = lat < n_lat - 1
    has_dn = lat > 0
    right = lax.rem(lon + 1, n_lon)
    left = lax.rem(lon + n_lon - 1, n_lon)
    up_id = {"lon": lon, "lat": lat + 1}
    dn_id = {"lon": lon, "lat": lat - 1}
    right_id = {"lon": right, "lat": lat}
    left_id = {"lon": left, "lat": lat}

    half = n_lon // 2
    place = lax.rem(lon, half)
    far_right = place == half - 1
    far_left = place == 0
    is_far = far_right | far_left
    is_near = jnp.logical_not(is_far)
    far = jnp.where(far_right, right, left)
    partner = jnp.where(far_right, left, right)
    by_right_end = place == half - 2
    by_left_end = place == 1
    is_partner = by_right_end | by_left_end
    end = jnp.where(by_right_end, right, left)
    late_half = lon >= half
    early_half = jnp.logical_not(late_half)

    def field_copy(f):
        return pltpu.make_async_copy(flat_hbm.at[f], q_buf.at[f], own_sem.at[f])

    c_copy = pltpu.make_async_copy(c_flat_hbm, c_buf, own_sem.at[nf])
    small = [
        pltpu.make_async_copy(source, target, small_sem.at[i])
        for i, (source, target) in enumerate(
            [
                (cosz_hbm, cosz_ref),
                (albedo_hbm, albedo_ref),
                (ext_hbm, ext_ref),
                (ssa_hbm, ssa_ref),
                (weight_hbm, weight_ref),
                (order_hbm, order_ref),
                (count_hbm, count_ref),
            ]
        )
    ]

    barrier = pltpu.get_barrier_semaphore()

    def greet(device):
        pl.semaphore_signal(barrier, inc=1, device_id=device, device_id_type=MESH)

    @pl.when(is_far)
    def _():
        greet({"lon": partner, "lat": lat})
        greet({"lon": far, "lat": lat})

        @pl.when(has_up)
        def _():
            greet({"lon": partner, "lat": lat + 1})

        @pl.when(has_dn)
        def _():
            greet({"lon": partner, "lat": lat - 1})

    @pl.when(is_near)
    def _():
        @pl.when(has_up)
        def _():
            greet(up_id)

        @pl.when(has_dn)
        def _():
            greet(dn_id)

        @pl.when(jnp.logical_not(by_right_end))
        def _():
            greet(right_id)

        @pl.when(jnp.logical_not(by_left_end))
        def _():
            greet(left_id)

    for f in range(nf):
        field_copy(f).start()
    c_copy.start()
    for copy in small:
        copy.start()

    n_beside = has_up.astype(jnp.int32) + has_dn.astype(jnp.int32)

    @pl.when(is_near)
    def _():
        pl.semaphore_wait(barrier, 2 + n_beside + jnp.where(is_partner, n_beside, 0))

        @pl.when(is_partner)
        def _():
            pl.semaphore_signal(
                go_sem, inc=1, device_id={"lon": end, "lat": lat}, device_id_type=MESH
            )

    @pl.when(is_far)
    def _():
        pl.semaphore_wait(go_sem, 1)

    def z1_copy(f, side, r):
        if side == 0:
            source, target, device = rows - HALO + r, r, up_id
        else:
            source, target, device = r, HALO + r, dn_id
        return pltpu.make_async_remote_copy(
            src_ref=fields_hbm.at[f, :, source, 0],
            dst_ref=q_halo.at[f, target],
            send_sem=z1_send.at[side, f, r],
            recv_sem=z1_recv.at[side, f, r],
            device_id=device,
            device_id_type=MESH,
        )

    def z2_copy(f, side):
        if side == 0:
            source, target, device = rows, 0, up_id
        else:
            source, target, device = HALO, HALO + rows, dn_id
        return pltpu.make_async_remote_copy(
            src_ref=s_buf.at[f, pl.ds(source, HALO)],
            dst_ref=s_buf.at[f, pl.ds(target, HALO)],
            send_sem=z2_send.at[side, f],
            recv_sem=z2_recv.at[side, f],
            device_id=device,
            device_id_type=MESH,
        )

    cn_copy = pltpu.make_async_remote_copy(
        src_ref=courant_hbm.at[1, :, rows - 1, 0],
        dst_ref=c_north.at[0],
        send_sem=cn_send,
        recv_sem=cn_recv,
        device_id=up_id,
        device_id_type=MESH,
    )

    def x1_copy(side):
        return pltpu.make_async_remote_copy(
            src_ref=send_1.at[side],
            dst_ref=recv_1.at[side],
            send_sem=x1_send.at[side],
            recv_sem=x1_recv.at[side],
            device_id=right_id if side == 0 else left_id,
            device_id_type=MESH,
        )

    def x2_copy(n, side):
        return pltpu.make_async_remote_copy(
            src_ref=send_2.at[side, n],
            dst_ref=recv_2.at[side, n],
            send_sem=x2_send.at[side, n],
            recv_sem=x2_recv.at[side, n],
            device_id=right_id if side == 0 else left_id,
            device_id_type=MESH,
        )

    @pl.when(has_up)
    def _():
        cn_copy.start()

    def z1_start(f):
        @pl.when(has_up)
        def _():
            for r in range(HALO):
                z1_copy(f, 0, r).start()

        @pl.when(has_dn)
        def _():
            for r in range(HALO):
                z1_copy(f, 1, r).start()

    early = jnp.where(is_partner & late_half, YIELD, nf)
    early = jnp.where(is_near, early, jnp.where(late_half, EARLY_SECOND, EARLY_FIRST))
    pl.loop(0, early)(z1_start)

    zero = jnp.zeros((8, lanes), jnp.float32)

    def fill_zero(ref):
        for g in range(groups):
            ref[pl.ds(8 * g, 8), :] = zero

    @pl.when(jnp.logical_not(has_dn))
    def _():
        fill_zero(c_north.at[0])

        @pl.loop(0, nf)
        def _(f):
            for r in range(HALO):
                fill_zero(q_halo.at[f, r])
                fill_zero(s_buf.at[f, r])

    @pl.when(jnp.logical_not(has_up))
    def _():
        @pl.loop(0, nf)
        def _(f):
            for r in range(HALO):
                fill_zero(q_halo.at[f, HALO + r])
                fill_zero(s_buf.at[f, HALO + rows + r])

    lane = lax.broadcasted_iota(jnp.int32, (8, lanes), 1)
    sub = lax.broadcasted_iota(jnp.int32, (8, lanes), 0)
    slot = lane >> 2
    own_half = (lane & 3) < 2
    low = sub < 4

    def pack(load):
        packed = zero
        for r in range(rows):
            for g in range(groups):
                k = r * groups + g
                packed = jnp.where(
                    slot == k, pltpu.roll(load(r, g), (4 * k + 2) % lanes, 1), packed
                )
        return packed

    def send_pair(buf, n, even, odd):
        buf[0, n] = jnp.where(own_half, even, pltpu.roll(odd, 2, 1))
        buf[1, n] = jnp.where(own_half, pltpu.roll(even, lanes - 2, 1), odd)

    def recv_pair(buf, n, odd):
        from_left = buf[0, n]
        from_right = buf[1, n]
        first = jnp.where(own_half, from_left, pltpu.roll(from_right, 2, 1))
        second = jnp.where(own_half, pltpu.roll(from_left, lanes - 2, 1), from_right)
        return jnp.where(odd, second, first)

    def own_row(f, r, g):
        return q_buf[f, pl.ds(8 * rows * g + r, 8, stride=rows), :]

    def courant_row(n, r, g):
        return c_buf[n, pl.ds(8 * rows * g + r, 8, stride=rows), :]

    @pl.loop(0, nf)
    def _(f):
        field_copy(f).wait()
        pack_q[f] = pack(lambda r, g: own_row(f, r, g))

    c_copy.wait()
    pairs_f = nf // 2
    c_pack = pack(lambda r, g: courant_row(0, r, g))
    for n in range(pairs_f):
        send_pair(send_1, n, pack_q[2 * n], pack_q[2 * n + 1])
    send_pair(send_1, pairs_f, c_pack, c_pack)
    c_edge[0] = c_pack * (1.0 / 12.0)

    for side in range(2):
        @pl.when(jnp.logical_not(far_right if side == 0 else far_left))
        def _():
            x1_copy(side).start()

    def send_far(where):
        @pl.when(where & is_far)
        def _():
            pl.semaphore_wait(barrier, 1)

        for side in range(2):
            @pl.when(where & (far_right if side == 0 else far_left))
            def _():
                x1_copy(side).start()

        @pl.when(where & is_far)
        def _():
            pl.loop(early, nf)(z1_start)

    send_far(late_half)

    ahead = lax.broadcasted_iota(jnp.int32, (2 * lanes, 2 * lanes), 0) & (lanes - 1)
    column = lax.broadcasted_iota(jnp.int32, (2 * lanes, 2 * lanes), 1)
    ahead = ahead - jnp.where(column < lanes, column, column - lanes - 1)
    inner = (ahead == 0) | (ahead == 1)
    outer = (ahead == -1) | (ahead == 2)
    band[...] = jnp.where(inner, 7.0, jnp.where(outer, -1.0, 0.0)).astype(jnp.bfloat16)

    for copy in small:
        copy.wait()
    cosz = jnp.concatenate([cosz_ref[...], cosz_ref[...]], axis=0)
    albedo = jnp.concatenate([albedo_ref[...], albedo_ref[...]], axis=0)
    neg_inv_mu = -1.0 / cosz
    ext = [
        jnp.where(low, ext_ref[2 * p], ext_ref[2 * p + 1]) * (4.0 / lev) for p in range(pairs)
    ]
    half_ssa = [jnp.where(low, ssa_ref[2 * p], ssa_ref[2 * p + 1]) * 0.5 for p in range(pairs)]
    weight = [jnp.where(low, weight_ref[2 * p], weight_ref[2 * p + 1]) for p in range(pairs)]

    ranks = lax.broadcasted_iota(jnp.int32, (lanes, lanes), 1)
    columns = lax.broadcasted_iota(jnp.int32, (lanes, lanes), 0)
    ones = jnp.ones((8, lanes), jnp.float32)
    sunlit = zero
    for r in range(rows):
        hit = (order_ref[r] == columns) & (ranks < count_ref[r])
        row = lax.dot_general(
            ones,
            hit.astype(jnp.float32),
            (((1,), (1,)), ((), ())),
            preferred_element_type=jnp.float32,
        )
        sunlit = jnp.where((sub & 3) == r, row, sunlit)
    sunlit = sunlit * float(lev)

    def optics(k, beam):
        raw = q_buf[1, pl.ds(pl.multiple_of(8 * k, 8), 8), :]
        water = jnp.maximum(raw, 0.0) + jnp.log1p(jnp.exp(-jnp.abs(raw)))
        turned = pltpu.roll(water, 4, 0)
        for half in range(2):
            level = 2 * k + half
            here = jnp.where(low, water, turned) if half == 0 else jnp.where(low, turned, water)
            after = []
            for p in range(pairs):
                tau = ext[p] * here
                direct = jnp.exp(tau * neg_inv_mu)
                decay = jnp.exp(tau * -1.66)
                rad_a[level, p] = decay
                rad_b[level, p] = half_ssa[p] * (beam[p] * (1.0 - direct))
                rad_g[level, p] = beam[p]
                after.append(beam[p] * direct)
            beam = tuple(after)
        return beam

    beam = lax.fori_loop(0, lev // 2, optics, tuple(cosz for _ in range(pairs)))

    def up_level(i, carry):
        level = lev - 1 - i
        a_below, b_below = carry
        a_out, b_out = [], []
        for p in range(pairs):
            decay = rad_a[level, p]
            source = rad_b[level, p]
            reflect = half_ssa[p] * (1.0 - decay)
            transmit = decay + reflect
            inv = 1.0 / (1.0 - reflect * a_below[p])
            through = transmit * inv
            a_here = reflect + transmit * through * a_below[p]
            b_here = through * (a_below[p] * source + b_below[p]) + source
            rad_a[level, p] = through
            rad_b[level, p] = (reflect * b_below[p] + source) * inv
            rad_c[level, p] = weight[p] * (1.0 - a_here)
            rad_g[level, p] = weight[p] * (rad_g[level, p] - b_here)
            a_out.append(a_here)
            b_out.append(b_here)
        return tuple(a_out), tuple(b_out)

    floor_b = tuple(albedo * beam[p] for p in range(pairs))
    for p in range(pairs):
        rad_c[lev, p] = weight[p] * (1.0 - albedo)
        rad_g[lev, p] = weight[p] * (beam[p] - floor_b[p])
    lax.fori_loop(0, lev, up_level, (tuple(albedo for _ in range(pairs)), floor_b))

    def net_flux(level, down):
        total = rad_c[level, 0] * down[0] + rad_g[level, 0]
        for p in range(1, pairs):
            total = total + (rad_c[level, p] * down[p] + rad_g[level, p])
        return total + pltpu.roll(total, 4, 0)

    def down_pair(k, carry):
        down, net = carry
        heats = []
        for half in range(2):
            level = 2 * k + half
            down = tuple(rad_a[level, p] * down[p] + rad_b[level, p] for p in range(pairs))
            below = net_flux(level + 1, down)
            heats.append((net - below) * sunlit)
            net = below
        heat_ref[pl.ds(pl.multiple_of(8 * k, 8), 8), :] = jnp.where(low, heats[0], heats[1])
        return down, net

    start = tuple(zero for _ in range(pairs))
    lax.fori_loop(0, lev // 2, down_pair, (start, net_flux(0, start)))
    send_far(early_half)

    @pl.when(is_partner)
    def _():
        pl.loop(early, nf)(z1_start)


    @pl.when(has_dn)
    def _():
        cn_copy.wait_recv()

    for r in range(rows):
        for g in range(groups):
            here = courant_row(0, r, g) * (1.0 / 12.0)
            c_east[r, pl.ds(8 * g, 8), :] = here
            c_west[r, pl.ds(8 * g, 8), :] = jnp.where(lane == 0, 0.0, pltpu.roll(here, 1, 1))
            c_north[r + 1, pl.ds(8 * g, 8), :] = courant_row(1, r, g) * (1.0 / 12.0)
    for g in range(groups):
        c_north[0, pl.ds(8 * g, 8), :] = c_north[0, pl.ds(8 * g, 8), :] * (1.0 / 12.0)

    def tendency(load, emit):
        x = jnp.concatenate(
            [load(HALO + r, g) for r in range(rows) for g in range(groups)], axis=0
        )
        upper = x.astype(jnp.bfloat16)
        lower = (x - upper.astype(jnp.float32)).astype(jnp.bfloat16)
        flux = jnp.dot(
            jnp.concatenate([upper, lower], axis=1),
            band[...],
            preferred_element_type=jnp.float32,
        )
        for g in range(groups):
            at = pl.ds(8 * g, 8)
            q = [load(j, g) for j in range(rows + 2 * HALO)]
            north = [
                c_north[j, at, :] * (7.0 * (q[j + 1] + q[j + 2]) - (q[j] + q[j + 3]))
                for j in range(rows + 1)
            ]
            for r in range(rows):
                k = r * groups + g
                east = c_east[r, at, :] * flux[8 * k : 8 * k + 8, :lanes]
                west = c_west[r, at, :] * flux[8 * k : 8 * k + 8, lanes:]
                emit(r, g, q[r + HALO], (north[r] - north[r + 1]) - (east - west))

    corner = lane & 3

    def edge(halo, own):
        m1 = pltpu.roll(halo, 1, 1)
        m2 = pltpu.roll(halo, 2, 1)
        p1 = pltpu.roll(halo, lanes - 1, 1)
        p2 = pltpu.roll(halo, lanes - 2, 1)
        beside = pltpu.roll(own, lanes - 1, 1)
        east = jnp.where(
            corner == 0,
            -p2,
            jnp.where(corner == 1, 7.0 * p1 - p2, jnp.where(corner == 2, -m1, 0.0)),
        )
        west = jnp.where(
            corner == 0,
            0.0,
            jnp.where(
                corner == 1,
                -p1,
                jnp.where(corner == 2, 7.0 * (m1 + own) - (m2 + beside), -m2),
            ),
        )
        return c_edge[1] * west - c_edge[0] * east

    edge_lanes = (lane < 2) | (lane >= lanes - 2)

    def spread(packed, k):
        return jnp.where(edge_lanes, pltpu.roll(packed, (lanes - 2 - 4 * k) % lanes, 1), 0.0)

    def x1_wait():
        x1_copy(0).wait_recv()
        x1_copy(1).wait_recv()
        beyond = recv_pair(recv_1, pairs_f, False) * (1.0 / 12.0)
        c_edge[1] = jnp.where(
            corner == 2, pltpu.roll(beyond, 1, 1), pltpu.roll(c_edge[0], 1, 1)
        )

    def z1_wait(f):
        @pl.when(has_dn)
        def _():
            for r in range(HALO):
                z1_copy(f, 0, r).wait_recv()

        @pl.when(has_up)
        def _():
            for r in range(HALO):
                z1_copy(f, 1, r).wait_recv()

    def add_edge(f):
        change = edge(recv_pair(recv_1, f // 2, f % 2 == 1), pack_q[f])
        edge_buf[f] = change
        pack_s[f] = pack_s[f] + change

        @pl.when(f % 2 == 1)
        def _():
            n = f // 2
            send_pair(send_2, n, pack_s[f - 1], pack_s[f])
            x2_copy(n, 0).start()
            x2_copy(n, 1).start()

    def spread_edge(f):
        change = edge_buf[f]
        for r in range(rows):
            for g in range(groups):
                at = pl.ds(8 * g, 8)
                s_buf[f, HALO + r, at, :] = s_buf[f, HALO + r, at, :] + spread(
                    change, r * groups + g
                )

    def z2_start(f):
        @pl.when(has_up)
        def _():
            z2_copy(f, 0).start()

        @pl.when(has_dn)
        def _():
            z2_copy(f, 1).start()

    pl.when(is_near)(x1_wait)
    held = nf - 2

    @pl.loop(0, nf)
    def _(f):
        z1_wait(f)

        def load(j, g):
            at = pl.ds(8 * g, 8)
            if j < HALO:
                return q_halo[f, j, at, :]
            if j < HALO + rows:
                return own_row(f, j - HALO, g)
            return q_halo[f, j - rows, at, :]

        parts = [zero] * rows

        def emit(r, g, here, change):
            k = r * groups + g
            value = here + change
            s_buf[f, HALO + r, pl.ds(8 * g, 8), :] = value
            parts[r] = jnp.where(slot == k, pltpu.roll(value, (4 * k + 2) % lanes, 1), parts[r])

        tendency(load, emit)
        pack_s[f] = sum(parts[1:], parts[0])

        @pl.when(is_near)
        def _():
            add_edge(f)
            spread_edge(f)
            z2_start(f)

        @pl.when(is_far & (f == held - 1))
        def _():
            x1_wait()
            pl.loop(0, held)(add_edge)
            pl.loop(0, held)(spread_edge)

        @pl.when(is_far & (f >= held))
        def _():
            add_edge(f)

    @pl.when(is_far)
    def _():
        pl.loop(0, held)(z2_start)

        @pl.loop(held, nf)
        def _(f):
            spread_edge(f)
            z2_start(f)

    def x2_wait(n):
        x2_copy(n, 0).wait_recv()
        x2_copy(n, 1).wait_recv()

    def z2_sent(f):
        @pl.when(has_up)
        def _():
            z2_copy(f, 0).wait_send()

        @pl.when(has_dn)
        def _():
            z2_copy(f, 1).wait_send()

    def second_edge(f):
        return edge(recv_pair(recv_2, f // 2, f % 2 == 1), pack_s[f])

    def out_rows(r, g):
        return pl.ds(8 * rows * g + r, 8, stride=rows)

    def z2_wait(f):
        @pl.when(has_dn)
        def _():
            z2_copy(f, 0).wait_recv()

        @pl.when(has_up)
        def _():
            z2_copy(f, 1).wait_recv()

    def final(f, load):
        beyond = second_edge(f)

        def emit(r, g, here, change):
            total = (own_row(f, r, g) + here) + (change + spread(beyond, r * groups + g))
            out_ref[f, out_rows(r, g), :] = 0.5 * total

        tendency(load, emit)

    @pl.loop(0, nf)
    def _(f):
        @pl.when(has_up)
        def _():
            for r in range(HALO):
                z1_copy(f, 0, r).wait_send()

        @pl.when(has_dn)
        def _():
            for r in range(HALO):
                z1_copy(f, 1, r).wait_send()

    @pl.when(has_up)
    def _():
        cn_copy.wait_send()

    for side in range(2):
        x1_copy(side).wait_send()

    @pl.loop(0, nf - 1)
    def _(f):
        @pl.when(f % 2 == 0)
        def _():
            x2_wait(f // 2)
            x2_copy(f // 2, 0).wait_send()
            x2_copy(f // 2, 1).wait_send()

        @pl.when(f > 0)
        def _():
            z2_sent(f - 1)

        z2_wait(f)
        final(f, lambda j, g: s_buf[f, j, pl.ds(8 * g, 8), :])

        @pl.when(f == 0)
        def _():
            for i in range(rows * groups):
                at = pl.ds(8 * i, 8)
                out_ref[0, at, :] = out_ref[0, at, :] + 0.5 * heat_ref[at, :]

    last = nf - 1

    def inner_row(j, g):
        if j < HALO or j >= HALO + rows:
            return zero
        return s_buf[last, j, pl.ds(8 * g, 8), :]

    z2_sent(last - 1)
    final(last, inner_row)
    z2_wait(last)
    top = HALO + rows
    for g in range(groups):
        at = pl.ds(8 * g, 8)
        below = s_buf[last, HALO - 1, at, :]
        above = s_buf[last, top, at, :]
        low_face = c_north[0, at, :] * (7.0 * below - s_buf[last, HALO - 2, at, :])
        high_face = c_north[rows, at, :] * (7.0 * above - s_buf[last, top + 1, at, :])
        low_next = c_north[1, at, :] * below
        high_next = c_north[rows - 1, at, :] * above
        terms = {0: low_face + low_next, 1: -low_next}
        for r, term in ((rows - 2, high_next), (rows - 1, -high_next - high_face)):
            terms[r] = terms[r] + term if r in terms else term
        for r in sorted(terms):
            rows_at = out_rows(r, g)
            out_ref[last, rows_at, :] = out_ref[last, rows_at, :] + 0.5 * terms[r]

    z2_sent(last)


def store_kernel(parts, new_ref, heat_ref, new_hbm, out_heat_hbm, sem):
    copies = [
        pltpu.make_async_copy(new_ref.at[f], new_hbm.at[f], sem.at[f]) for f in range(parts)
    ]
    copies.append(pltpu.make_async_copy(heat_ref, out_heat_hbm, sem.at[parts]))
    for copy in copies:
        copy.start()
    for copy in copies:
        copy.wait()


def per_device(n_lat, n_lon, fields, courant, cosz, albedo, ext, ssa, weight, order, count):
    nf, lev, rows, lanes = fields.shape
    bands = ext.shape[0]
    dims = (nf, lev, rows, lanes, bands, n_lat, n_lon)
    tall = rows + 2 * HALO
    f32 = jnp.float32
    hbm_spec = pl.BlockSpec(memory_space=pltpu.HBM)
    vmem_spec = pl.BlockSpec(memory_space=pltpu.VMEM)
    rad = pltpu.VMEM((lev + 1, bands // 2, 8, lanes), f32)
    pairs_f = nf // 2
    results = (
        jax.ShapeDtypeStruct((nf, lev * rows, lanes), f32),
        jax.ShapeDtypeStruct((lev * rows, lanes), f32),
    )
    out, heat = pl.pallas_call(
        functools.partial(step_kernel, dims),
        out_shape=(
            pltpu.VMEM((nf, lev * rows, lanes), f32),
            pltpu.VMEM((lev * rows, lanes), f32),
        ),
        in_specs=[hbm_spec] * 11,
        out_specs=(vmem_spec, vmem_spec),
        scratch_shapes=[
            pltpu.VMEM((nf, lev * rows, lanes), f32),
            pltpu.VMEM((nf, 2 * HALO, lev, lanes), f32),
            pltpu.VMEM((nf, tall, lev, lanes), f32),
            pltpu.VMEM((2, lev * rows, lanes), f32),
            pltpu.VMEM((rows, lev, lanes), f32),
            pltpu.VMEM((rows, lev, lanes), f32),
            pltpu.VMEM((rows + 1, lev, lanes), f32),
            pltpu.VMEM((rows, lanes), f32),
            pltpu.VMEM((rows, lanes), f32),
            pltpu.SMEM((bands,), f32),
            pltpu.SMEM((bands,), f32),
            pltpu.SMEM((bands,), f32),
            pltpu.VMEM((rows, 1, lanes), jnp.int32),
            pltpu.SMEM((rows,), jnp.int32),
            rad,
            rad,
            rad,
            rad,
            pltpu.VMEM((2 * lanes, 2 * lanes), jnp.bfloat16),
            pltpu.VMEM((2, 8, lanes), f32),
            pltpu.VMEM((nf, 8, lanes), f32),
            pltpu.VMEM((nf, 8, lanes), f32),
            pltpu.VMEM((nf, 8, lanes), f32),
            pltpu.VMEM((2, pairs_f + 1, 8, lanes), f32),
            pltpu.VMEM((2, pairs_f + 1, 8, lanes), f32),
            pltpu.VMEM((2, pairs_f, 8, lanes), f32),
            pltpu.VMEM((2, pairs_f, 8, lanes), f32),
            pltpu.SemaphoreType.DMA((nf + 1,)),
            pltpu.SemaphoreType.DMA((7,)),
            pltpu.SemaphoreType.REGULAR,
            pltpu.SemaphoreType.DMA((2, nf, HALO)),
            pltpu.SemaphoreType.DMA((2, nf, HALO)),
            pltpu.SemaphoreType.DMA((2, nf)),
            pltpu.SemaphoreType.DMA((2, nf)),
            pltpu.SemaphoreType.DMA,
            pltpu.SemaphoreType.DMA,
            pltpu.SemaphoreType.DMA((2,)),
            pltpu.SemaphoreType.DMA((2,)),
            pltpu.SemaphoreType.DMA((2, pairs_f)),
            pltpu.SemaphoreType.DMA((2, pairs_f)),
        ],
        compiler_params=pltpu.CompilerParams(
            collective_id=0, has_side_effects=True, vmem_limit_bytes=48 * 1024 * 1024
        ),
        name="advect_radiate",
    )(
        *(
            pltpu.with_memory_space_constraint(x, pltpu.HBM)
            for x in (
                fields.reshape(nf, lev, rows, 1, lanes),
                fields.reshape(nf, lev * rows, lanes),
                courant.reshape(2, lev, rows, 1, lanes),
                courant.reshape(2, lev * rows, lanes),
                cosz,
                albedo,
                ext,
                ssa,
                weight,
                order,
                count.reshape(rows),
            )
        )
    )
    out, heat = pl.pallas_call(
        functools.partial(store_kernel, nf),
        out_shape=results,
        in_specs=[pl.BlockSpec(memory_space=pl.ANY)] * 2,
        out_specs=(hbm_spec, hbm_spec),
        scratch_shapes=[pltpu.SemaphoreType.DMA((nf + 1,))],
        compiler_params=pltpu.CompilerParams(vmem_limit_bytes=32 * 1024 * 1024),
        name="store_results",
    )(out, heat)
    return out.reshape(nf, lev, rows, lanes), heat.reshape(lev, rows, lanes)


def solution(mesh):
    n_lat, n_lon = mesh.shape["lat"], mesh.shape["lon"]
    in_specs = (
        P(None, None, "lat", "lon"),
        P(None, None, "lat", "lon"),
        P("lat", "lon"),
        P("lat", "lon"),
        P(),
        P(),
        P(),
        P("lat", "lon", None),
        P("lat", "lon"),
    )
    out_specs = (P(None, None, "lat", "lon"), P(None, "lat", "lon"))
    return jax.shard_map(
        functools.partial(per_device, n_lat, n_lon),
        mesh=mesh,
        in_specs=in_specs,
        out_specs=out_specs,
        check_vma=False,
    )
```
